256 devices in a mesh: queue: 64 (over z, y, x_lo), mp: 4 (over x_hi, core).
Axes of the slice: x: 4 (x_hi: 2, x_lo: 2; x = x_hi * 2 + x_lo), y: 4, z: 8, core: 2. Of those that a mesh axis runs over, the one named last changes fastest.
Arguments:
- state: bfloat16 [64, 512, 3072], P('queue', None, 'mp')
- key_cache: bfloat16 [64, 32, 3072], P('queue', None, 'mp'), as said below
- value_cache: bfloat16 [64, 32, 3072], P('queue', None, 'mp'), may hold values from -15 to 15
- level_gain: float32 [50, 3072], P(None, 'mp'), may hold values from 0.25 to 1.75
- sigma: float32 [51], replicated, may hold values from 0.05 to 1.5
- levels: int32 [64], P('queue'), may hold values from 0 to 49
- group_len: int32 [64], replicated, may hold values from 256 to 512, as said below
- ctx_ids: int32 [64, 6], P('queue'), may hold values from 0 to 62, as said below
- ctx_count: int32 [64], P('queue'), may hold values from 0 to 6, as said below
Outputs:
- advanced: bfloat16 [64, 512, 3072], P('queue', None, 'mp')
The draws below stay inside these ranges and needn't reach their ends.
Inputs may be any that keep to these rules, and one draw needn't show every extreme that they name: `group_len`: some group has exactly 512 live tokens. `ctx_count`: slot c lists at most min(c, 6) blocks, and the last slot lists exactly 6. `ctx_ids`: the first ctx_count[c] entries of slot c are distinct blocks of index below c; the other entries are 0. `key_cache`: keys of the clean context blocks.
All inputs are finite; a program needn't handle non-finite values.
Results may differ from the reference program's by a relative error of at most 0.015.
The reference program's roundings to bfloat16 on the way (of `current`, `queries`, `own_keys`, `rounded` and `updated`) count: a program that leaves them out, or rounds other values in their place, can miss the bound.
Values may be sent and summed in bfloat16 or wider, within the bound.
A program may use at most 64 MiB of HBM per device.

```python
import math
import jax
import jax.numpy as jnp
from jax import lax

HEADS = 24
HEAD_DIM = 128
FEAT = 3072
CT = 512
CB = 32
NB = 6
LEVELS = 50
STEPS = 2
GROUPS = 64


def draw_state(key, part):
    first_key, second_key, third_key = jax.random.split(key, 3)
    shape_all = (GROUPS, CT, FEAT)
    base_draw = jax.random.normal(first_key, shape_all, jnp.float32)
    feature_index = jnp.arange(FEAT).astype(jnp.float32)
    column_scale = jnp.exp(0.5 * math.log(3.0) * (feature_index / FEAT - 0.5))
    column_scale = column_scale * jnp.exp(jax.random.uniform(second_key, (FEAT,), jnp.float32, -1.15, 1.15))
    row_scale = jnp.exp(jax.random.uniform(third_key, (GROUPS, CT, 1), jnp.float32, -1.15, 1.15))
    drawn = 0.3 * base_draw * column_scale * row_scale
    return drawn.astype(jnp.bfloat16)


def draw_key_cache(key, part):
    shape_all = (GROUPS, CB, FEAT)
    drawn = jax.random.normal(key, shape_all, jnp.float32)
    return drawn.astype(jnp.bfloat16)


def draw_group_len(key, part):
    first_key, second_key = jax.random.split(key, 2)
    lengths = jax.random.randint(first_key, (GROUPS,), CT // 2, CT + 1)
    fullest = jax.random.randint(second_key, (), 0, GROUPS)
    return jnp.where(jnp.arange(GROUPS) == fullest, CT, lengths).astype(jnp.int32)


def context_counts(key):
    slot_index = jnp.arange(GROUPS)
    wanted = jax.random.randint(jax.random.fold_in(key, 11), (GROUPS,), 1, NB + 1)
    counts = jnp.minimum(slot_index, wanted)
    return jnp.where(slot_index == GROUPS - 1, NB, counts).astype(jnp.int32)


def draw_ctx_count(key, part):
    return context_counts(key)


def draw_ctx_ids(key, part):
    counts = context_counts(key)
    raw_priority = jax.random.randint(jax.random.fold_in(key, 12), (GROUPS, GROUPS), 0, GROUPS)
    slot_index = jnp.arange(GROUPS)[:, None]
    block_index = jnp.arange(GROUPS)[None, :]
    priority = raw_priority + (GROUPS - block_index) // 2 + 2 * GROUPS * (block_index == slot_index - 1)
    priority = jnp.where(block_index < slot_index, priority, -1)
    priority = priority * GROUPS + block_index
    unused, picked = lax.top_k(priority, NB)
    listed = jnp.where(jnp.arange(NB)[None, :] < counts[:, None], picked, 0)
    return listed.astype(jnp.int32)


def plant(array, rng, smallest, top_value):
    spot = [jax.random.randint(jax.random.fold_in(rng, axis), (), 0, length) for axis, length in enumerate(array.shape)]
    widest = array.shape.index(max(array.shape))
    beside = spot[:widest] + [(spot[widest] + 1) % array.shape[widest]] + spot[widest + 1:]
    return array.at[tuple(spot)].set(smallest).at[tuple(beside)].set(top_value)


def block_scale(stream_key, dims, cuts, smallest, high):
    def one(position, blocks):
        steps = jax.random.uniform(jax.random.fold_in(jax.random.fold_in(stream_key, 6), position), (blocks,), jnp.float32, smallest / len(cuts), high / len(cuts))
        return jnp.repeat(jnp.exp(steps), dims[position] // blocks).reshape((-1,) + (1,) * (len(dims) - position - 1))

    loudness = one(*cuts[0])
    for cut in cuts[1:]:
        loudness = loudness * one(*cut)
    return loudness


def centred(rng, dims, scale, reach, shards=(), kind=jnp.bfloat16):
    values = jax.random.normal(rng, dims, jnp.float32) * scale
    if len(shards) > 0:
        values = block_scale(rng, dims, shards, -0.22, 0.18) * values
    return jnp.clip(values, min=-reach, max=reach).astype(kind)


def setup_inputs(seed: int = 0) -> dict:
    keys = jax.random.split(jax.random.key(seed), 10)
    return {
        "state": draw_state(jax.random.fold_in(keys[9], 71), 0),
        "key_cache": draw_key_cache(jax.random.fold_in(keys[9], 71), 0),
        "value_cache": centred(keys[2], (GROUPS, CB, FEAT), 2.5, 15.0, ((0, 64), (2, 4))),
        "level_gain": jnp.clip(1.0 + 0.15 * jax.random.normal(keys[3], (LEVELS, FEAT), jnp.float32), 0.25, 1.75),
        "sigma": jnp.clip(jnp.exp(jax.random.uniform(keys[4], (LEVELS + 1,), jnp.float32, math.log(0.05), math.log(1.5))), 0.05, 1.5),
        "levels": plant(jax.random.randint(keys[5], (GROUPS,), 0, LEVELS), jax.random.fold_in(keys[5], 1), 0, LEVELS - 1).astype(jnp.int32),
        "group_len": draw_group_len(jax.random.fold_in(keys[9], 71), 0),
        "ctx_ids": draw_ctx_ids(jax.random.fold_in(keys[9], 71), 0),
        "ctx_count": draw_ctx_count(jax.random.fold_in(keys[9], 71), 0),
    }


def attend(queries, all_keys, all_values, key_live, scaling):
    scores = jnp.einsum('rhd,khd->hrk', queries.astype(jnp.float32), all_keys.astype(jnp.float32)) * scaling
    scores = jnp.where(key_live[None, None, :], scores, -jnp.inf)
    row_max = lax.optimization_barrier(jnp.max(scores, axis=-1, keepdims=True))
    weights = jnp.exp(scores - row_max)
    totals = lax.optimization_barrier(jnp.sum(weights, axis=-1))
    rounded = weights.astype(jnp.bfloat16)
    weighted = jnp.einsum('hrk,khd->rhd', rounded.astype(jnp.float32), all_values.astype(jnp.float32))
    return weighted / jnp.transpose(totals)[:, :, None]

def reference(state, key_cache, value_cache, level_gain, sigma, levels, group_len, ctx_ids, ctx_count):
    row_count = state.shape[1]
    scaling = HEAD_DIM ** (-0.5)
    step_sizes = sigma[levels + 1] - sigma[levels]
    level_gains = level_gain[levels]
    current = state
    for step_index in range(STEPS):
        lengths = jnp.roll(group_len, step_index)
        widened = current.astype(jnp.float32)
        mean_square = lax.optimization_barrier(jnp.mean(widened * widened, axis=-1, keepdims=True))
        normed = widened * lax.rsqrt(mean_square + 1e-06)
        queries = (normed * level_gains[:, None, :]).astype(jnp.bfloat16)
        own_keys = normed.astype(jnp.bfloat16)

        def per_group(inputs):
            query_rows, key_rows, own_values, block_list, list_count, length, step_size = inputs
            context_keys = key_cache[block_list].reshape(NB * CB, FEAT)
            context_values = value_cache[block_list].reshape(NB * CB, FEAT)
            all_keys = jnp.concatenate([key_rows, context_keys], axis=0)
            all_values = jnp.concatenate([own_values, context_values], axis=0)
            token_live = jnp.arange(row_count) < length
            block_live = jnp.repeat(jnp.arange(NB) < list_count, CB)
            key_live = jnp.concatenate([token_live, block_live], axis=0)
            attended = attend(query_rows.reshape(row_count, HEADS, HEAD_DIM), all_keys.reshape(-1, HEADS, HEAD_DIM), all_values.reshape(-1, HEADS, HEAD_DIM), key_live, scaling)
            attended = attended.reshape(row_count, FEAT)
            widened_own = own_values.astype(jnp.float32)
            advanced_rows = jnp.where(token_live[:, None], widened_own + step_size * attended, widened_own)
            return advanced_rows.astype(jnp.bfloat16)
        updated = lax.map(per_group, (queries, own_keys, current, ctx_ids, ctx_count, lengths, step_sizes))
        current = jnp.roll(updated, 1, axis=0)
    return current
```

```python
import functools
import math

import jax
import jax.numpy as jnp
from jax import lax
from jax.experimental import pallas as pl
from jax.experimental.pallas import tpu as pltpu
from jax.sharding import PartitionSpec as P

HEAD_DIM = 128
FEAT = 3072
MESH = pl.DeviceIdType.MESH
NZ, NY = 8, 4
PAIRS = NZ * NY
ROWS = 256


def plan():
    def onward(item):
        a, dz, dy, part = item
        if a == 0:
            if dy == 0:
                if -3 < dz <= 0:
                    yield "z+", (a, dz - 1, 0, part)
                if 0 <= dz < 3:
                    yield "z-", (a, dz + 1, 0, part)
                if dz == -3:
                    yield "z+", (a, -4, 0, 0)
                if dz == 3:
                    yield "z-", (a, 4, 0, 1)
                yield "y-", (a, dz, 1, part)
                yield "y+", (a, dz, -1, part)
            elif dy == 1:
                yield "y-", (a, dz, 2, part)
        else:
            if dz == 0 and dy == 0:
                yield "y-", (a, 0, 1, part)
                yield "y+", (a, 0, -1, part)
            if dz == 0 and dy == 1:
                yield "y-", (a, 0, 2, part)
            if -3 < dz <= 0 or (dz == -3 and dy in (0, 1)):
                yield "z+", (a, dz - 1, dy, part)
            if 0 <= dz < 3 or (dz == 3 and dy in (-1, 2)):
                yield "z-", (a, dz + 1, dy, part)

    held, steps = [(0, 0, 0, None), (1, 0, 0, None)], []
    while held:
        arrived = []
        for item in held:
            out = list(onward(item))
            steps.append((item, out))
            arrived.extend(got for _, got in out)
        held = arrived
    return steps


STEPS = plan()
SENT = [got for _, out in STEPS for _, got in out]
NUMBER = {got: i for i, got in enumerate(SENT)}


def kernel(
    state, key, value, gain, sigma, lengths, level_in, count_in, ids_in,
    out,
    kbuf, vbuf, st, st2, ck, cv, inv, sq, parts, meta, meta_s, stage,
    sem_local, sem_meta, sem_state, sem_x, sem_send, sem_recv, sem_sq, sem_out,
):
    q, p = lax.axis_index("queue"), lax.axis_index("mp")
    xl, m = q % 2, q // 2
    y, z = m % NY, m // NY
    half = 3 * HEAD_DIM
    mine = pl.multiple_of(xl * half, HEAD_DIM)
    other = pl.multiple_of((1 - xl) * half, HEAD_DIM)
    me = p * 2 + xl
    after, before = (m + 1) % PAIRS, (m + PAIRS - 1) % PAIRS

    def at(pair, x, mp=None):
        return {"queue": pair * 2 + x, "mp": p if mp is None else mp}

    to = {
        "z+": at(((z + 1) % NZ) * NY + y, xl),
        "z-": at(((z + NZ - 1) % NZ) * NY + y, xl),
        "y+": at(z * NY + (y + 1) % NY, xl),
        "y-": at(z * NY + (y + NY - 1) % NY, xl),
    }
    partner = at(m, 1 - xl)
    peers = []
    for k in range(1, 8):
        e = (me + k) % 8
        peers.append(at(m, e % 2, e // 2))

    barrier = pltpu.get_barrier_semaphore()
    greeted = [*to.values(), *peers, at(after, 0), at(after, 1), at(before, 0), at(before, 1)]
    for d in greeted:
        pl.semaphore_signal(barrier, inc=1, device_id=d, device_id_type=MESH)

    lane = lax.broadcasted_iota(jnp.int32, (8, 128), 1)
    tile = jnp.where(lane == 0, level_in[0], jnp.where(lane == 1, count_in[0], 0))
    for k in range(6):
        tile = jnp.where(lane == 2 + k, ids_in[0, k], tile)
    meta[2 + xl] = tile

    own = [
        pltpu.make_async_copy(key.at[:, pl.ds(mine, half)], kbuf.at[q], sem_local.at[0]),
        pltpu.make_async_copy(value.at[:, pl.ds(mine, half)], vbuf.at[q], sem_local.at[1]),
    ]
    for c in own:
        c.start()
    pl.semaphore_wait(barrier, len(greeted))

    def remote(src, dst, send, recv, device):
        return pltpu.make_async_remote_copy(
            src_ref=src, dst_ref=dst, send_sem=send, recv_sem=recv, device_id=device, device_id_type=MESH
        )

    swapped = [
        remote(key.at[:, pl.ds(other, half)], kbuf.at[q], sem_x.at[0, 0], sem_x.at[1, 0], partner),
        remote(value.at[:, pl.ds(other, half)], vbuf.at[q], sem_x.at[0, 1], sem_x.at[1, 1], partner),
    ]
    for c in swapped:
        c.start()
    listed = [
        remote(meta.at[2 + xl], meta.at[xl], sem_meta.at[0, 0], sem_meta.at[1, xl], at(after, 0)),
        remote(meta.at[2 + xl], meta.at[xl], sem_meta.at[0, 1], sem_meta.at[1, xl], at(after, 1)),
        remote(meta.at[2 + xl], meta.at[2 + xl], sem_meta.at[0, 2], sem_meta.at[1, 2], partner),
    ]
    for c in listed:
        c.start()
    moved = [
        remote(state.at[:, f * half : (f + 1) * half], st.at[xl], sem_state.at[0, f], sem_state.at[1, xl], at(after, f))
        for f in range(2)
    ]
    for c in moved:
        c.start()

    for c in own:
        c.wait()
    theirs = 2 * m + 1 - xl
    for i, buf in enumerate((kbuf, vbuf)):
        remote(buf.at[theirs], buf.at[theirs], sem_x.at[0, i], sem_x.at[1, i], partner).wait_recv()

    def region(item):
        a, dz, dy, part = item
        buf = vbuf if a else kbuf
        pair = ((z + dz + NZ) % NZ) * NY + (y + dy + NY) % NY
        return buf.at[pl.ds(pair * 2, 2)] if part is None else buf.at[pl.ds(pair * 2 + part, 1)]

    flying = []
    for item, out_items in STEPS:
        if item in NUMBER:
            n = NUMBER[item]
            here = region(item)
            remote(here, here, sem_send.at[n], sem_recv.at[n], to["y+"]).wait_recv()
        for way, got in out_items:
            n = NUMBER[got]
            src = region((item[0], item[1], item[2], got[3]))
            c = remote(src, src, sem_send.at[n], sem_recv.at[n], to[way])
            c.start()
            flying.append(c)

    for j in range(2):
        remote(meta.at[j], meta.at[j], sem_meta.at[0, 0], sem_meta.at[1, j], partner).wait_recv()
    remote(meta.at[3 - xl], meta.at[3 - xl], sem_meta.at[0, 2], sem_meta.at[1, 2], partner).wait_recv()
    for c in listed:
        c.wait_send()
    into_s = pltpu.make_async_copy(meta, meta_s, sem_local.at[2])
    into_s.start()
    into_s.wait()
    for j in range(2):
        remote(st.at[j], st.at[j], sem_state.at[0, 0], sem_state.at[1, j], partner).wait_recv()

    row8 = lax.broadcasted_iota(jnp.int32, (8, 128), 0)

    def totals(step):
        mine8 = jnp.zeros((8, 128), jnp.float32)
        for r in range(8):
            piece = sq[r // 4, (r % 4) * 128 : (r % 4 + 1) * 128, :]
            line = jnp.sum(jnp.transpose(piece), axis=0, keepdims=True)
            mine8 = jnp.where(row8 == r, jnp.broadcast_to(line, (8, 128)), mine8)
        parts[step, me] = mine8
        out_going = []
        for k in range(1, 8):
            c = remote(
                parts.at[step, me], parts.at[step, me],
                sem_sq.at[0, step, k], sem_sq.at[1, step, k], peers[k - 1],
            )
            c.start()
            out_going.append(c)
        for k in range(1, 8):
            e = (me + 8 - k) % 8
            remote(
                parts.at[step, e], parts.at[step, e],
                sem_sq.at[0, step, k], sem_sq.at[1, step, k], peers[k - 1],
            ).wait_recv()
        whole = parts[step, 0]
        for e in range(1, 8):
            whole = whole + parts[step, e]
        factor = lax.rsqrt(whole / FEAT + 1e-06)
        for r in range(8):
            wide = jnp.broadcast_to(factor[r : r + 1, :], (128, 128))
            inv[r // 4, (r % 4) * 128 : (r % 4 + 1) * 128, :] = jnp.transpose(wide)
        return out_going

    scale = HEAD_DIM ** (-0.5) * math.log2(math.e)
    nt = (((1,), (1,)), ((), ()))

    def unit(source, step, j, h, store):
        level = meta_s[j + step, 0, 0]
        count = meta_s[j + step, 0, 1]
        length = lengths[(2 * m + 62 + j) % 64]
        columns = pl.ds(pl.multiple_of(h * HEAD_DIM, HEAD_DIM), HEAD_DIM)
        table = gain[:, pl.ds(pl.multiple_of(mine + h * HEAD_DIM, HEAD_DIM), HEAD_DIM)]
        level_row = lax.broadcasted_iota(jnp.int32, table.shape, 0)
        gains = jnp.sum(jnp.where(level_row == level, table, 0.0), axis=0, keepdims=True)
        size = sigma[level + 1] - sigma[level]
        keys = (source[j, :, columns].astype(jnp.float32) * inv[j]).astype(jnp.bfloat16)
        values = source[j, :, columns]
        more_keys, more_values = ck[:, columns], cv[:, columns]
        own_lane = lax.broadcasted_iota(jnp.int32, (1, 512), 1)
        more_lane = lax.broadcasted_iota(jnp.int32, (1, 192), 1)
        own_bias = jnp.where(own_lane < length, 0.0, -jnp.inf)
        more_bias = jnp.where(more_lane < count * 32, 0.0, -jnp.inf)
        for b in range(512 // ROWS):
            rows = pl.ds(b * ROWS, ROWS)
            x = source[j, rows, columns].astype(jnp.float32)
            queries = (x * inv[j, rows, :] * gains).astype(jnp.bfloat16)
            s1 = lax.dot_general(queries, keys, nt, preferred_element_type=jnp.float32) + own_bias
            s2 = lax.dot_general(queries, more_keys, nt, preferred_element_type=jnp.float32) + more_bias
            top = jnp.maximum(jnp.max(s1, axis=1, keepdims=True), jnp.max(s2, axis=1, keepdims=True))
            w1 = jnp.exp2((s1 - top) * scale)
            w2 = jnp.exp2((s2 - top) * scale)
            total = jnp.sum(w1, axis=1, keepdims=True) + jnp.sum(w2, axis=1, keepdims=True)
            o = jnp.dot(w1.astype(jnp.bfloat16), values, preferred_element_type=jnp.float32)
            o = o + jnp.dot(w2.astype(jnp.bfloat16), more_values, preferred_element_type=jnp.float32)
            live = lax.broadcasted_iota(jnp.int32, (ROWS, 1), 0) + b * ROWS < length
            store(rows, columns, jnp.where(live, x + size * (o * (1.0 / total)), x).astype(jnp.bfloat16))

    def fetch(step, j):
        for k in range(6):
            block = meta_s[j + step, 0, 2 + k]
            ck[k * 32 : (k + 1) * 32, :] = kbuf[block]
            cv[k * 32 : (k + 1) * 32, :] = vbuf[block]

    def squared(source, j, h):
        x = source[j, :, pl.ds(pl.multiple_of(h * HEAD_DIM, HEAD_DIM), HEAD_DIM)].astype(jnp.float32)
        sq[j] = sq[j] + x * x

    sq[...] = jnp.zeros_like(sq)

    @pl.loop(0, 6)
    def _(u):
        squared(st, u // 3, u % 3)

    ends = totals(0)
    sq[...] = jnp.zeros_like(sq)

    @pl.loop(0, 2)
    def _(j):
        fetch(0, j)

        @pl.loop(0, 3)
        def _(h):
            def store(rows, columns, new):
                st2[j, rows, columns] = new
                wide = new.astype(jnp.float32)
                sq[j, rows, :] = sq[j, rows, :] + wide * wide

            unit(st, 0, j, h, store)

    ends += totals(1)

    far = 1 - xl
    fetch(1, far)

    def crossing(h):
        place = pl.ds(pl.multiple_of(mine + h * HEAD_DIM, HEAD_DIM), HEAD_DIM)
        return remote(stage.at[h], out.at[:, place], sem_out.at[0, h], sem_out.at[1, h], partner)

    @pl.loop(0, 3)
    def _(h):
        def store(rows, columns, new):
            stage[h, rows, :] = new

        unit(st2, 1, far, h, store)
        crossing(h).start()

    fetch(1, xl)

    @pl.loop(0, 3)
    def _(h):
        def store(rows, columns, new):
            out[rows, pl.ds(pl.multiple_of(mine + h * HEAD_DIM, HEAD_DIM), HEAD_DIM)] = new

        unit(st2, 1, xl, h, store)

    for c in swapped + moved + flying + ends:
        c.wait_send()
    for h in range(3):
        place = pl.ds(pl.multiple_of(other + h * HEAD_DIM, HEAD_DIM), HEAD_DIM)
        crossing(h).wait_send()
        remote(stage.at[h], out.at[:, place], sem_out.at[0, h], sem_out.at[1, h], partner).wait_recv()


def on_device(state, key_cache, value_cache, level_gain, sigma, levels, group_len, ctx_ids, ctx_count):
    vmem, smem, anywhere = (
        pl.BlockSpec(memory_space=pltpu.VMEM),
        pl.BlockSpec(memory_space=pltpu.SMEM),
        pl.BlockSpec(memory_space=pl.ANY),
    )
    half = 3 * HEAD_DIM
    copies = len(SENT)
    dma = pltpu.SemaphoreType.DMA
    done = pl.pallas_call(
        kernel,
        name="queue_steps",
        out_shape=jax.ShapeDtypeStruct(state.shape[1:], jnp.bfloat16),
        in_specs=[anywhere, anywhere, anywhere, vmem, smem, smem, smem, smem, smem],
        out_specs=vmem,
        scratch_shapes=[
            pltpu.VMEM((64, 32, half), jnp.bfloat16),
            pltpu.VMEM((64, 32, half), jnp.bfloat16),
            pltpu.VMEM((2, 512, half), jnp.bfloat16),
            pltpu.VMEM((2, 512, half), jnp.bfloat16),
            pltpu.VMEM((192, half), jnp.bfloat16),
            pltpu.VMEM((192, half), jnp.bfloat16),
            pltpu.VMEM((2, 512, 128), jnp.float32),
            pltpu.VMEM((2, 512, 128), jnp.float32),
            pltpu.VMEM((2, 8, 8, 128), jnp.float32),
            pltpu.VMEM((4, 8, 128), jnp.int32),
            pltpu.SMEM((4, 8, 128), jnp.int32),
            pltpu.VMEM((3, 512, 128), jnp.bfloat16),
            dma((3,)),
            dma((2, 3)),
            dma((2, 2)),
            dma((2, 2)),
            dma((copies,)),
            dma((copies,)),
            dma((2, 2, 8)),
            dma((2, 3)),
        ],
        compiler_params=pltpu.CompilerParams(
            collective_id=0, has_side_effects=True, vmem_limit_bytes=48 << 20
        ),
    )(state[0], key_cache[0], value_cache[0], level_gain, sigma, group_len, levels, ctx_count, ctx_ids)
    return done[None]


def solution(mesh):
    in_specs = (
        P("queue", None, "mp"),
        P("queue", None, "mp"),
        P("queue", None, "mp"),
        P(None, "mp"),
        P(),
        P("queue"),
        P(),
        P("queue", None),
        P("queue"),
    )
    return jax.shard_map(
        on_device, mesh=mesh, in_specs=in_specs, out_specs=P("queue", None, "mp"), check_vma=False
    )
```

```python
import functools
import math

import jax
import jax.numpy as jnp
from jax import lax
from jax.experimental import pallas as pl
from jax.experimental.pallas import tpu as pltpu
from jax.sharding import PartitionSpec as P

HEAD_DIM = 128
FEAT = 3072
MESH = pl.DeviceIdType.MESH
NZ, NY = 8, 4
PAIRS = NZ * NY
ROWS = 256
CHUNK = 64
EARLY, EVERY = 2, 2
RELAYED = 2


def plan():
    def onward(item):
        a, dz, dy, part = item
        if a == 0:
            if dy == 0:
                if -3 < dz <= 0:
                    yield "z+", (a, dz - 1, 0, part)
                if 0 <= dz < 3:
                    yield "z-", (a, dz + 1, 0, part)
                if dz == -3:
                    yield "z+", (a, -4, 0, 0)
                if dz == 3:
                    yield "z-", (a, 4, 0, 1)
                yield "y-", (a, dz, 1, part)
                yield "y+", (a, dz, -1, part)
            elif dy == 1:
                yield "y-", (a, dz, 2, part)
        else:
            if dz == 0 and dy == 0:
                yield "y-", (a, 0, 1, part)
                yield "y+", (a, 0, -1, part)
            if dz == 0 and dy == 1:
                yield "y-", (a, 0, 2, part)
            if -3 < dz <= 0 or (dz == -3 and dy in (0, 1)):
                yield "z+", (a, dz - 1, dy, part)
            if 0 <= dz < 3 or (dz == 3 and dy in (-1, 2)):
                yield "z-", (a, dz + 1, dy, part)

    held, steps = [(0, 0, 0, None), (1, 0, 0, None)], []
    while held:
        arrived = []
        for item in held:
            out = list(onward(item))
            steps.append((item, out))
            arrived.extend(got for _, got in out)
        held = arrived
    return steps


STEPS = plan()
SENT = [got for _, out in STEPS for _, got in out]
NUMBER = {got: i for i, got in enumerate(SENT)}


def kernel(
    state, key, value, gain_in, sigma_in, lengths_in, levels_in, counts_in, lists_in,
    out,
    kbuf, vbuf, st, st2, ck, cv, inv, sq, parts, meta, meta_s, stage, relay, gain,
    sigma, lengths, level_in, count_in, ids_in,
    sem_local, sem_small, sem_meta, sem_state, sem_x, sem_send, sem_recv, sem_sq, sem_out, sem_relay,
):
    q, p = lax.axis_index("queue"), lax.axis_index("mp")
    xl, m = q % 2, q // 2
    y, z = m % NY, m // NY
    half = 3 * HEAD_DIM
    mine = pl.multiple_of(xl * half, HEAD_DIM)
    other = pl.multiple_of((1 - xl) * half, HEAD_DIM)
    me = p * 2 + xl
    after, before = (m + 1) % PAIRS, (m + PAIRS - 1) % PAIRS
    up, down = z * NY + (y + 1) % NY, z * NY + (y + NY - 1) % NY
    over, under = ((z + 1) % NZ) * NY + y, ((z + NZ - 1) % NZ) * NY + y

    def at(pair, x, mp=None):
        return {"queue": pair * 2 + x, "mp": p if mp is None else mp}

    to = {
        "z+": at(over, xl),
        "z-": at(under, xl),
        "y+": at(up, xl),
        "y-": at(down, xl),
    }
    partner = at(m, 1 - xl)
    peers = []
    for k in range(1, 8):
        e = (me + k) % 8
        peers.append(at(m, e % 2, e // 2))

    barrier = pltpu.get_barrier_semaphore()
    greeted = [*peers, *(at(pair, x) for pair in (up, down, over, under, after, before) for x in range(2))]
    for d in greeted:
        pl.semaphore_signal(barrier, inc=1, device_id=d, device_id_type=MESH)

    small = [
        pltpu.make_async_copy(a, b, sem_small.at[i])
        for i, (a, b) in enumerate(
            [(levels_in, level_in), (counts_in, count_in), (lists_in, ids_in),
             (sigma_in, sigma), (lengths_in, lengths), (gain_in, gain)]
        )
    ]
    for c in small:
        c.start()
    own = [
        pltpu.make_async_copy(key.at[:, pl.ds(mine, half)], kbuf.at[q], sem_local.at[0]),
        pltpu.make_async_copy(value.at[:, pl.ds(mine, half)], vbuf.at[q], sem_local.at[1]),
    ]
    for c in own:
        c.start()
    for c in small:
        c.wait()

    lane = lax.broadcasted_iota(jnp.int32, (8, 128), 1)
    tile = jnp.where(lane == 0, level_in[0], jnp.where(lane == 1, count_in[0], 0))
    for k in range(6):
        tile = jnp.where(lane == 2 + k, ids_in[0, k], tile)
    meta[2 + xl] = tile

    pl.semaphore_wait(barrier, len(greeted))

    def remote(src, dst, send, recv, device):
        return pltpu.make_async_remote_copy(
            src_ref=src, dst_ref=dst, send_sem=send, recv_sem=recv, device_id=device, device_id_type=MESH
        )

    swapped = [
        remote(key.at[:, pl.ds(other, half)], kbuf.at[q], sem_x.at[0, 0], sem_x.at[1, 0], partner),
        remote(value.at[:, pl.ds(other, half)], vbuf.at[q], sem_x.at[0, 1], sem_x.at[1, 1], partner),
    ]
    for c in swapped:
        c.start()
    mine_here = meta.at[2 + xl]
    listed = [
        remote(mine_here, meta.at[row + xl], sem_meta.at[0, i], sem_meta.at[1, row + xl], d)
        for i, (row, d) in enumerate(
            [(0, at(up, 0)), (0, at(up, 1)), (2, partner), (4, at(before, 0)), (4, at(before, 1))]
        )
    ]
    for c in listed:
        c.start()
    def part_of(f, i):
        return state.at[pl.ds(i * CHUNK, CHUNK), f * half : (f + 1) * half]

    chunks = range(512 // CHUNK)
    rising = [
        [remote(part_of(f, i), st.at[0, pl.ds(i * CHUNK, CHUNK)], sem_state.at[0, f, i], sem_state.at[1, 0, i], at(up, f)) for f in range(2)]
        for i in chunks
    ]
    across = [
        remote(part_of(0, i), st.at[1, pl.ds(i * CHUNK, CHUNK)], sem_state.at[0, 0, i], sem_state.at[1, 1, i], partner)
        for i in chunks
    ]
    staying = pltpu.make_async_copy(state.at[:, half:], st.at[1], sem_local.at[3])

    @pl.when(xl == 1)
    def _():
        staying.start()

    def move(i):
        @pl.when(xl == 0)
        def _():
            for c in rising[i]:
                c.start()

        @pl.when(xl == 1)
        def _():
            across[i].start()

    for c in own:
        c.wait()
    theirs = 2 * m + 1 - xl
    for i, buf in enumerate((kbuf, vbuf)):
        remote(buf.at[theirs], buf.at[theirs], sem_x.at[0, i], sem_x.at[1, i], partner).wait_recv()

    def region(item):
        a, dz, dy, part = item
        buf = vbuf if a else kbuf
        pair = ((z + dz + NZ) % NZ) * NY + (y + dy + NY) % NY
        return buf.at[pl.ds(pair * 2, 2)] if part is None else buf.at[pl.ds(pair * 2 + part, 1)]

    flying, waiting = [], list(chunks)
    last = max(i for i, (_, out_items) in enumerate(STEPS) if out_items)

    def arrived(item):
        if item in NUMBER:
            n = NUMBER[item]
            here = region(item)
            remote(here, here, sem_send.at[n], sem_recv.at[n], to["y+"]).wait_recv()

    for i, (item, out_items) in enumerate(STEPS[: last + 1]):
        arrived(item)
        for way, got in out_items:
            n = NUMBER[got]
            src = region((item[0], item[1], item[2], got[3]))
            c = remote(src, src, sem_send.at[n], sem_recv.at[n], to[way])
            c.start()
            flying.append(c)
        if waiting and i >= EARLY and (i - EARLY) % EVERY == 0:
            move(waiting.pop(0))
    for i in waiting:
        move(i)

    for row in (0, 1, 3 - xl, 4, 5):
        remote(meta.at[row], meta.at[row], sem_meta.at[0, 0], sem_meta.at[1, row], partner).wait_recv()
    for c in listed:
        c.wait_send()
    into_s = pltpu.make_async_copy(meta, meta_s, sem_local.at[2])
    into_s.start()
    into_s.wait()
    row8 = lax.broadcasted_iota(jnp.int32, (8, 128), 0)
    ends = []

    def tell(step, j):
        mine8 = jnp.zeros((8, 128), jnp.float32)
        for r in range(4):
            piece = sq[j, r * 128 : (r + 1) * 128, :]
            line = jnp.sum(jnp.transpose(piece), axis=0, keepdims=True)
            mine8 = jnp.where(row8 == r, jnp.broadcast_to(line, (8, 128)), mine8)
        parts[step, j, me] = mine8
        for k in range(1, 8):
            c = remote(
                parts.at[step, j, me], parts.at[step, j, me],
                sem_sq.at[0, step, j, k], sem_sq.at[1, step, j, k], peers[k - 1],
            )
            c.start()
            ends.append(c)

    def hear(step, j):
        for k in range(1, 8):
            e = (me + 8 - k) % 8
            remote(
                parts.at[step, j, e], parts.at[step, j, e],
                sem_sq.at[0, step, j, k], sem_sq.at[1, step, j, k], peers[k - 1],
            ).wait_recv()
        whole = parts[step, j, 0]
        for e in range(1, 8):
            whole = whole + parts[step, j, e]
        factor = lax.rsqrt(whole / FEAT + 1e-06)
        for r in range(4):
            wide = jnp.broadcast_to(factor[r : r + 1, :], (128, 128))
            inv[j, r * 128 : (r + 1) * 128, :] = jnp.transpose(wide)

    scale = HEAD_DIM ** (-0.5) * math.log2(math.e)
    nt = (((1,), (1,)), ((), ()))

    def unit(source, step, j, h, store):
        level = meta_s[3 * j + step, 0, 0]
        count = meta_s[3 * j + step, 0, 1]
        length = lengths[2 * m + 1 if j else 2 * down]
        columns = pl.ds(pl.multiple_of(h * HEAD_DIM, HEAD_DIM), HEAD_DIM)
        table = gain[:, pl.ds(pl.multiple_of(mine + h * HEAD_DIM, HEAD_DIM), HEAD_DIM)]
        level_row = lax.broadcasted_iota(jnp.int32, table.shape, 0)
        gains = jnp.sum(jnp.where(level_row == level, table, 0.0), axis=0, keepdims=True)
        size = sigma[level + 1] - sigma[level]
        keys = (source[j, :, columns].astype(jnp.float32) * inv[j]).astype(jnp.bfloat16)
        values = source[j, :, columns]
        more_keys, more_values = ck[:, columns], cv[:, columns]
        own_lane = lax.broadcasted_iota(jnp.int32, (1, 512), 1)
        more_lane = lax.broadcasted_iota(jnp.int32, (1, 192), 1)
        own_bias = jnp.where(own_lane < length, 0.0, -jnp.inf)
        more_bias = jnp.where(more_lane < count * 32, 0.0, -jnp.inf)
        for b in range(512 // ROWS):
            rows = pl.ds(b * ROWS, ROWS)
            x = source[j, rows, columns].astype(jnp.float32)
            queries = (x * inv[j, rows, :] * gains).astype(jnp.bfloat16)
            s1 = lax.dot_general(queries, keys, nt, preferred_element_type=jnp.float32) + own_bias
            s2 = lax.dot_general(queries, more_keys, nt, preferred_element_type=jnp.float32) + more_bias
            top = jnp.maximum(jnp.max(s1, axis=1, keepdims=True), jnp.max(s2, axis=1, keepdims=True))
            w1 = jnp.exp2((s1 - top) * scale)
            w2 = jnp.exp2((s2 - top) * scale)
            total = jnp.sum(w1, axis=1, keepdims=True) + jnp.sum(w2, axis=1, keepdims=True)
            o = jnp.dot(w1.astype(jnp.bfloat16), values, preferred_element_type=jnp.float32)
            o = o + jnp.dot(w2.astype(jnp.bfloat16), more_values, preferred_element_type=jnp.float32)
            live = lax.broadcasted_iota(jnp.int32, (ROWS, 1), 0) + b * ROWS < length
            store(rows, columns, jnp.where(live, x + size * (o * (1.0 / total)), x).astype(jnp.bfloat16))

    def fetch(step, j):
        for k in range(6):
            block = meta_s[3 * j + step, 0, 2 + k]
            ck[k * 32 : (k + 1) * 32, :] = kbuf[block]
            cv[k * 32 : (k + 1) * 32, :] = vbuf[block]

    def landed(j):
        for i in chunks:
            here = st.at[j, pl.ds(i * CHUNK, CHUNK)]
            remote(here, here, sem_state.at[0, 0, i], sem_state.at[1, j, i], partner).wait_recv()

    for j in (1, 0):
        if j == 0:
            landed(0)
        else:
            pl.when(xl == 0)(functools.partial(landed, 1))
            pl.when(xl == 1)(staying.wait)

        @pl.loop(0, 4)
        def _(b, j=j):
            rows = pl.ds(b * 128, 128)
            x = st[j, rows, :].astype(jnp.float32)
            x = x * x
            sq[j, rows, :] = x[:, :128] + x[:, 128:256] + x[:, 256:]

        tell(0, j)
    for item, _ in STEPS[last + 1 :]:
        arrived(item)

    for j in (1, 0):
        hear(0, j)
        fetch(0, j)
        sq[j] = jnp.zeros((512, 128), jnp.float32)

        @pl.loop(0, 3)
        def _(h, j=j):
            def store(rows, columns, new):
                st2[j, rows, columns] = new
                wide = new.astype(jnp.float32)
                sq[j, rows, :] = sq[j, rows, :] + wide * wide

            unit(st, 0, j, h, store)

        tell(1, j)

    def place(f, h):
        return out.at[:, pl.ds(pl.multiple_of(f * half + h * HEAD_DIM, HEAD_DIM), HEAD_DIM)]

    def send(j, h, device):
        return remote(stage.at[j, h], place(xl, h), sem_out.at[0, j, h], sem_out.at[1, xl, h], device)

    def to_relay(h):
        return remote(stage.at[1, h], relay.at[h], sem_out.at[0, 1, h], sem_relay.at[1, h], at(after, 0))

    def from_relay(h):
        return remote(relay.at[h], place(0, h), sem_relay.at[0, h], sem_out.at[1, 0, h], partner)

    def received(f, h):
        remote(stage.at[0, h], place(f, h), sem_out.at[0, 0, h], sem_out.at[1, f, h], partner).wait_recv()

    turned = (y == 0).astype(jnp.int32)
    group0_leaves = (xl == 1) | (y == 0)
    home = at(m + turned * (over - m), 0)
    hear(1, 1)
    fetch(1, 1)

    @pl.loop(0, 3)
    def _(h):
        def store(rows, columns, new):
            stage[1, h, rows, :] = new

        unit(st2, 1, 1, h, store)
        relayed = (xl == 0) & (h < RELAYED)

        @pl.when(relayed)
        def _():
            to_relay(h).start()

        @pl.when(jnp.logical_not(relayed))
        def _():
            send(1, h, at(after, 1)).start()

    hear(1, 0)
    fetch(1, 0)

    @pl.loop(0, 3)
    def _(h):
        def store(rows, columns, new):
            stage[0, h, rows, :] = new

        unit(st2, 1, 0, h, store)

        @pl.when(group0_leaves)
        def _():
            send(0, h, home).start()

        @pl.when(jnp.logical_not(group0_leaves))
        def _():
            out[:, pl.ds(pl.multiple_of(h * HEAD_DIM, HEAD_DIM), HEAD_DIM)] = stage[0, h]

    @pl.when(xl == 0)
    def _():
        for h in range(RELAYED):
            to_relay(h).wait_recv()
            from_relay(h).start()

    for c in swapped + flying + ends:
        c.wait_send()
    for h in range(3):
        send(1, h, at(after, 1)).wait_send()

    @pl.when(group0_leaves)
    def _():
        for h in range(3):
            send(0, h, home).wait_send()

    @pl.when(xl == 0)
    def _():
        for pair in rising:
            for c in pair:
                c.wait_send()
        for h in range(RELAYED):
            from_relay(h).wait_send()
        for h in range(3):
            received(1, h)

    @pl.when((xl == 0) & (y == 0))
    def _():
        for h in range(3):
            received(0, h)

    @pl.when(xl == 1)
    def _():
        for c in across:
            c.wait_send()
        for h in range(3):
            received(0, h)
            received(1, h)


def on_device(state, key_cache, value_cache, level_gain, sigma, levels, group_len, ctx_ids, ctx_count):
    hbm = pl.BlockSpec(memory_space=pltpu.HBM)
    half = 3 * HEAD_DIM
    copies = len(SENT)
    dma = pltpu.SemaphoreType.DMA
    done = pl.pallas_call(
        kernel,
        name="queue_steps",
        out_shape=jax.ShapeDtypeStruct(state.shape[1:], jnp.bfloat16),
        in_specs=[hbm] * 9,
        out_specs=pl.BlockSpec(memory_space=pltpu.VMEM),
        scratch_shapes=[
            pltpu.VMEM((64, 32, half), jnp.bfloat16),
            pltpu.VMEM((64, 32, half), jnp.bfloat16),
            pltpu.VMEM((2, 512, half), jnp.bfloat16),
            pltpu.VMEM((2, 512, half), jnp.bfloat16),
            pltpu.VMEM((192, half), jnp.bfloat16),
            pltpu.VMEM((192, half), jnp.bfloat16),
            pltpu.VMEM((2, 512, 128), jnp.float32),
            pltpu.VMEM((2, 512, 128), jnp.float32),
            pltpu.VMEM((2, 2, 8, 8, 128), jnp.float32),
            pltpu.VMEM((6, 8, 128), jnp.int32),
            pltpu.SMEM((6, 8, 128), jnp.int32),
            pltpu.VMEM((2, 3, 512, 128), jnp.bfloat16),
            pltpu.VMEM((RELAYED, 512, 128), jnp.bfloat16),
            pltpu.VMEM(level_gain.shape, jnp.float32),
            pltpu.SMEM(sigma.shape, jnp.float32),
            pltpu.SMEM(group_len.shape, jnp.int32),
            pltpu.SMEM(levels.shape, jnp.int32),
            pltpu.SMEM(ctx_count.shape, jnp.int32),
            pltpu.SMEM(ctx_ids.shape, jnp.int32),
            dma((4,)),
            dma((6,)),
            dma((2, 6)),
            dma((2, 2, 512 // CHUNK)),
            dma((2, 2)),
            dma((copies,)),
            dma((copies,)),
            dma((2, 2, 2, 8)),
            dma((2, 2, 3)),
            dma((2, RELAYED)),
        ],
        compiler_params=pltpu.CompilerParams(
            collective_id=0, has_side_effects=True, vmem_limit_bytes=60 << 20
        ),
    )(state[0], key_cache[0], value_cache[0], level_gain, sigma, group_len, levels, ctx_count, ctx_ids)
    return done[None]


def solution(mesh):
    in_specs = (
        P("queue", None, "mp"),
        P("queue", None, "mp"),
        P("queue", None, "mp"),
        P(None, "mp"),
        P(),
        P("queue"),
        P(),
        P("queue", None),
        P("queue"),
    )
    return jax.shard_map(
        on_device, mesh=mesh, in_specs=in_specs, out_specs=P("queue", None, "mp"), check_vma=False
    )
```

```python
import functools
import math

import jax
import jax.numpy as jnp
from jax import lax
from jax.experimental import pallas as pl
from jax.experimental.pallas import tpu as pltpu
from jax.sharding import PartitionSpec as P

HEAD_DIM = 128
FEAT = 3072
MESH = pl.DeviceIdType.MESH
NZ, NY = 8, 4
PAIRS = NZ * NY
ROWS = 256
CHUNK = 64
EARLY, EVERY = 0, 6
LISTS_AT, TELL_AT, HEAR_AT = 6, 20, 40
RELAYED = 2


def plan():
    def onward(item):
        a, dz, dy, part = item
        if a == 0:
            if dy == 0:
                if -3 < dz <= 0:
                    yield "z+", (a, dz - 1, 0, part)
                if 0 <= dz < 3:
                    yield "z-", (a, dz + 1, 0, part)
                if dz == -2:
                    yield "z+2", (a, -4, 0, 0)
                if dz == 2:
                    yield "z-2", (a, 4, 0, 1)
                yield "y-", (a, dz, 1, part)
                yield "y+", (a, dz, -1, part)
            elif dy == 1:
                yield "y-", (a, dz, 2, part)
        else:
            if dz == 0 and dy == 0:
                yield "y-", (a, 0, 1, part)
                yield "y+", (a, 0, -1, part)
                yield "y2", (a, 0, 2, part)
            if -3 < dz <= 0 or (dz == -3 and dy in (0, 1)):
                yield "z+", (a, dz - 1, dy, part)
            if 0 <= dz < 3 or (dz == 3 and dy in (-1, 2)):
                yield "z-", (a, dz + 1, dy, part)

    held, steps = [(0, 0, 0, None), (1, 0, 0, None)], []
    while held:
        arrived = []
        for item in held:
            out = list(onward(item))
            steps.append((item, out))
            arrived.extend(got for _, got in out)
        held = arrived
    return steps


STEPS = plan()
SENT = [got for _, out in STEPS for _, got in out]
NUMBER = {got: i for i, got in enumerate(SENT)}
SECOND = {got: len(SENT) + i for i, got in enumerate(got for _, out in STEPS[:2] for _, got in out)}


def kernel(
    state, key, value, gain_in, sigma_in, lengths_in, levels_in, counts_in, lists_in,
    out,
    kbuf, vbuf, st, st2, ck, cv, inv, sq, parts, meta, meta_s, stage, relay, gain,
    sigma, lengths, level_in, count_in, ids_in,
    sem_local, sem_small, sem_meta, sem_state, sem_x, sem_send, sem_recv, sem_sq, sem_out, sem_relay,
):
    q, p = lax.axis_index("queue"), lax.axis_index("mp")
    xl, m = q % 2, q // 2
    y, z = m % NY, m // NY
    half = 3 * HEAD_DIM
    mine = pl.multiple_of(xl * half, HEAD_DIM)
    other = pl.multiple_of((1 - xl) * half, HEAD_DIM)
    me = p * 2 + xl
    after, before = (m + 1) % PAIRS, (m + PAIRS - 1) % PAIRS
    up, down = z * NY + (y + 1) % NY, z * NY + (y + NY - 1) % NY
    over, under = ((z + 1) % NZ) * NY + y, ((z + NZ - 1) % NZ) * NY + y

    def at(pair, x, mp=None):
        return {"queue": pair * 2 + x, "mp": p if mp is None else mp}

    pair_at = {
        "z+": over,
        "z-": under,
        "z+2": ((z + 2) % NZ) * NY + y,
        "z-2": ((z + NZ - 2) % NZ) * NY + y,
        "y+": up,
        "y-": down,
        "y2": z * NY + (y + 2) % NY,
    }
    to = {way: at(pair, xl) for way, pair in pair_at.items()}
    beside = {way: at(pair, 1 - xl) for way, pair in pair_at.items()}
    partner = at(m, 1 - xl)
    peers = []
    for k in range(1, 8):
        e = (me + k) % 8
        peers.append(at(m, e % 2, e // 2))

    barrier = pltpu.get_barrier_semaphore()
    greeted = [*peers, *(at(pair, x) for pair in (*pair_at.values(), after, before) for x in range(2))]
    for d in greeted:
        pl.semaphore_signal(barrier, inc=1, device_id=d, device_id_type=MESH)

    small = [
        pltpu.make_async_copy(a, b, sem_small.at[i])
        for i, (a, b) in enumerate(
            [(levels_in, level_in), (counts_in, count_in), (lists_in, ids_in),
             (sigma_in, sigma), (lengths_in, lengths), (gain_in, gain)]
        )
    ]
    for c in small:
        c.start()
    own = [
        pltpu.make_async_copy(key.at[:, pl.ds(mine, half)], kbuf.at[q], sem_local.at[0]),
        pltpu.make_async_copy(value.at[:, pl.ds(mine, half)], vbuf.at[q], sem_local.at[1]),
    ]
    for c in own:
        c.start()
    for c in small:
        c.wait()

    lane = lax.broadcasted_iota(jnp.int32, (8, 128), 1)
    tile = jnp.where(lane == 0, level_in[0], jnp.where(lane == 1, count_in[0], 0))
    for k in range(6):
        tile = jnp.where(lane == 2 + k, ids_in[0, k], tile)
    meta[2 + xl] = tile

    pl.semaphore_wait(barrier, len(greeted))

    def remote(src, dst, send, recv, device):
        return pltpu.make_async_remote_copy(
            src_ref=src, dst_ref=dst, send_sem=send, recv_sem=recv, device_id=device, device_id_type=MESH
        )

    swapped = [
        remote(key.at[:, pl.ds(other, half)], kbuf.at[q], sem_x.at[0, 0], sem_x.at[1, 0], partner),
        remote(value.at[:, pl.ds(other, half)], vbuf.at[q], sem_x.at[0, 1], sem_x.at[1, 1], partner),
    ]
    mine_here = meta.at[2 + xl]
    listed = [
        remote(mine_here, meta.at[row + xl], sem_meta.at[0, i], sem_meta.at[1, row + xl], d)
        for i, (row, d) in enumerate(
            [(0, at(up, 0)), (0, at(up, 1)), (2, partner), (4, at(before, 0)), (4, at(before, 1))]
        )
    ]
    def part_of(f, i):
        return state.at[pl.ds(i * CHUNK, CHUNK), f * half : (f + 1) * half]

    chunks = range(512 // CHUNK)
    rising = [
        [remote(part_of(f, i), st.at[0, pl.ds(i * CHUNK, CHUNK)], sem_state.at[0, f, i], sem_state.at[1, 0, i], at(up, f)) for f in range(2)]
        for i in chunks
    ]
    across = [
        remote(part_of(0, i), st.at[1, pl.ds(i * CHUNK, CHUNK)], sem_state.at[0, 0, i], sem_state.at[1, 1, i], partner)
        for i in chunks
    ]
    staying = pltpu.make_async_copy(state.at[:, half:], st.at[1], sem_local.at[3])

    def move(i):
        @pl.when(xl == 0)
        def _():
            for c in rising[i]:
                c.start()

    def region(item):
        a, dz, dy, part = item
        buf = vbuf if a else kbuf
        pair = ((z + dz + NZ) % NZ) * NY + (y + dy + NY) % NY
        return buf.at[pl.ds(pair * 2, 2)] if part is None else buf.at[pl.ds(pair * 2 + part, 1)]

    bufs, flying = (kbuf, vbuf), []
    theirs = 2 * m + 1 - xl
    for c in listed:
        c.start()
    for (item, out_items), source in zip(STEPS[:2], (key, value)):
        for way, got in out_items:
            for side, numbers, device in ((mine, NUMBER, to[way]), (other, SECOND, beside[way])):
                c = remote(
                    source.at[:, pl.ds(side, half)], bufs[item[0]].at[q],
                    sem_send.at[numbers[got]], sem_recv.at[numbers[got]], device,
                )
                c.start()
                flying.append(c)
    for c in swapped:
        c.start()

    @pl.when(xl == 1)
    def _():
        staying.start()
        for c in across:
            c.start()

    for c in own:
        c.wait()
    for i, buf in enumerate(bufs):
        remote(buf.at[theirs], buf.at[theirs], sem_x.at[0, i], sem_x.at[1, i], partner).wait_recv()

    def landed(j):
        for i in chunks:
            here = st.at[j, pl.ds(i * CHUNK, CHUNK)]
            remote(here, here, sem_state.at[0, 0, i], sem_state.at[1, j, i], partner).wait_recv()

    def squares(j):
        @pl.loop(0, 4)
        def _(b):
            rows = pl.ds(b * 128, 128)
            x = st[j, rows, :].astype(jnp.float32)
            x = x * x
            sq[j, rows, :] = x[:, :128] + x[:, 128:256] + x[:, 256:]

    row8 = lax.broadcasted_iota(jnp.int32, (8, 128), 0)
    ends = []

    def tell(step, j):
        mine8 = jnp.zeros((8, 128), jnp.float32)
        for r in range(4):
            piece = sq[j, r * 128 : (r + 1) * 128, :]
            line = jnp.sum(jnp.transpose(piece), axis=0, keepdims=True)
            mine8 = jnp.where(row8 == r, jnp.broadcast_to(line, (8, 128)), mine8)
        parts[step, j, me] = mine8
        for k in range(1, 8):
            c = remote(
                parts.at[step, j, me], parts.at[step, j, me],
                sem_sq.at[0, step, j, k], sem_sq.at[1, step, j, k], peers[k - 1],
            )
            c.start()
            ends.append(c)

    def hear(step, j):
        for k in range(1, 8):
            e = (me + 8 - k) % 8
            remote(
                parts.at[step, j, e], parts.at[step, j, e],
                sem_sq.at[0, step, j, k], sem_sq.at[1, step, j, k], peers[k - 1],
            ).wait_recv()
        whole = parts[step, j, 0]
        for e in range(1, 8):
            whole = whole + parts[step, j, e]
        factor = lax.rsqrt(whole / FEAT + 1e-06)
        for r in range(4):
            wide = jnp.broadcast_to(factor[r : r + 1, :], (128, 128))
            inv[j, r * 128 : (r + 1) * 128, :] = jnp.transpose(wide)

    def read_lists():
        for row in (0, 1, 3 - xl, 4, 5):
            remote(meta.at[row], meta.at[row], sem_meta.at[0, 0], sem_meta.at[1, row], partner).wait_recv()
        for c in listed:
            c.wait_send()
        into_s = pltpu.make_async_copy(meta, meta_s, sem_local.at[2])
        into_s.start()
        into_s.wait()

    waiting = list(chunks)
    last = max(i for i, (_, out_items) in enumerate(STEPS) if out_items)

    def arrived(item):
        if item in NUMBER:
            n = NUMBER[item]
            here = region(item)
            if item in SECOND:
                for slot, n in ((xl, n), (1 - xl, SECOND[item])):
                    one = here.at[pl.ds(slot, 1)]
                    remote(one, one, sem_send.at[n], sem_recv.at[n], to["y+"]).wait_recv()
            else:
                remote(here, here, sem_send.at[n], sem_recv.at[n], to["y+"]).wait_recv()

    for i, (item, out_items) in enumerate(STEPS[: last + 1]):
        arrived(item)
        for way, got in out_items if i > 1 else ():
            n = NUMBER[got]
            src = region((item[0], item[1], item[2], got[3]))
            c = remote(src, src, sem_send.at[n], sem_recv.at[n], to[way])
            c.start()
            flying.append(c)
        if i == LISTS_AT:
            read_lists()
        if i == TELL_AT:
            pl.when(xl == 0)(functools.partial(landed, 1))
            pl.when(xl == 1)(staying.wait)
            squares(1)
            tell(0, 1)
        if i == HEAR_AT:
            hear(0, 1)
        if waiting and i >= EARLY and (i - EARLY) % EVERY == 0:
            move(waiting.pop(0))
    for i in waiting:
        move(i)

    scale = HEAD_DIM ** (-0.5) * math.log2(math.e)
    nt = (((1,), (1,)), ((), ()))

    def fetch(step, j):
        for k in range(6):
            block = meta_s[3 * j + step, 0, 2 + k]
            ck[k * 32 : (k + 1) * 32, :] = kbuf[block]
            cv[k * 32 : (k + 1) * 32, :] = vbuf[block]

    def at_head(source, step, j, h):
        level = meta_s[3 * j + step, 0, 0]
        length = lengths[2 * m + 1 if j else 2 * down]
        columns = pl.ds(pl.multiple_of(h * HEAD_DIM, HEAD_DIM), HEAD_DIM)
        table = gain[:, pl.ds(pl.multiple_of(mine + h * HEAD_DIM, HEAD_DIM), HEAD_DIM)]
        level_row = lax.broadcasted_iota(jnp.int32, table.shape, 0)
        gains = jnp.sum(jnp.where(level_row == level, table, 0.0), axis=0, keepdims=True)
        keys = (source[j, :, columns].astype(jnp.float32) * inv[j]).astype(jnp.bfloat16)
        return columns, keys, gains, length

    def own_scores(source, j, rows, columns, keys, gains, length):
        x = source[j, rows, columns].astype(jnp.float32)
        queries = (x * inv[j, rows, :] * gains).astype(jnp.bfloat16)
        lane = lax.broadcasted_iota(jnp.int32, (1, 256), 1) + 256
        bias = jnp.where(lane < length, 0.0, -jnp.inf)
        s0 = lax.dot_general(queries, keys[:256], nt, preferred_element_type=jnp.float32)
        s1 = lax.dot_general(queries, keys[256:], nt, preferred_element_type=jnp.float32) + bias
        return queries, s0, s1

    def more_scores(queries, step, j, columns):
        lane = lax.broadcasted_iota(jnp.int32, (1, 192), 1)
        bias = jnp.where(lane < meta_s[3 * j + step, 0, 1] * 32, 0.0, -jnp.inf)
        return lax.dot_general(queries, ck[:, columns], nt, preferred_element_type=jnp.float32) + bias

    def highest(*scores):
        tops = [jnp.max(a, axis=1, keepdims=True) for a in scores]
        return functools.reduce(jnp.maximum, tops)

    def weighted(top, *terms):
        total, o = 0.0, 0.0
        for a, values in terms:
            w = jnp.exp2((a - top) * scale)
            total = total + jnp.sum(w, axis=1, keepdims=True)
            o = o + jnp.dot(w.astype(jnp.bfloat16), values, preferred_element_type=jnp.float32)
        return total, o

    def advanced(source, step, j, b, rows, columns, length, total, o):
        level = meta_s[3 * j + step, 0, 0]
        size = sigma[level + 1] - sigma[level]
        x = source[j, rows, columns].astype(jnp.float32)
        live = lax.broadcasted_iota(jnp.int32, (ROWS, 1), 0) + b * ROWS < length
        return jnp.where(live, x + size * (o * (1.0 / total)), x).astype(jnp.bfloat16)

    BLOCKS = [(b, slice(b * ROWS, (b + 1) * ROWS)) for b in range(512 // ROWS)]

    def whole_pass(source, step, j, finish):
        fetch(step, j)

        @pl.loop(0, 3)
        def _(h):
            columns, keys, gains, length = at_head(source, step, j, h)
            for b, rows in BLOCKS:
                queries, s0, s1 = own_scores(source, j, rows, columns, keys, gains, length)
                s2 = more_scores(queries, step, j, columns)
                top = highest(s0, s1, s2)
                total, o = weighted(
                    top, (s0, source[j, :256, columns]), (s1, source[j, 256:, columns]), (s2, cv[:, columns])
                )
                finish(h, b, rows, advanced(source, step, j, b, rows, columns, length, total, o))

    landed(0)
    squares(0)
    tell(0, 0)
    for item, _ in STEPS[last + 1 :]:
        arrived(item)
    def keep(j):
        def finish(h, b, rows, new):
            columns = pl.ds(pl.multiple_of(h * HEAD_DIM, HEAD_DIM), HEAD_DIM)
            st2[j, rows, columns] = new
            wide = new.astype(jnp.float32)
            sq[j, rows, :] = sq[j, rows, :] + wide * wide

        return finish

    for j in (1, 0):
        if j == 0:
            hear(0, 0)
        sq[j] = jnp.zeros((512, 128), jnp.float32)
        whole_pass(st, 0, j, keep(j))
        tell(1, j)

    def place(f, h, rows):
        return out.at[rows, pl.ds(pl.multiple_of(f * half + h * HEAD_DIM, HEAD_DIM), HEAD_DIM)]

    def send(j, h, b, rows, device):
        return remote(stage.at[j, h, rows], place(xl, h, rows), sem_out.at[0, j, h, b], sem_out.at[1, xl, h, b], device)

    def to_relay(h, b, rows):
        return remote(stage.at[1, h, rows], relay.at[h, rows], sem_out.at[0, 1, h, b], sem_relay.at[1, h, b], at(after, 0))

    def from_relay(h, b, rows):
        return remote(relay.at[h, rows], place(0, h, rows), sem_relay.at[0, h, b], sem_out.at[1, 0, h, b], partner)

    def received(f, h, b, rows):
        here = place(f, h, rows)
        remote(stage.at[0, h, rows], here, sem_out.at[0, 0, h, b], sem_out.at[1, f, h, b], partner).wait_recv()

    pieces = [(h, b, rows) for h in range(3) for b, rows in BLOCKS]

    turned = (y == 0).astype(jnp.int32)
    group0_leaves = (xl == 1) | (y == 0)
    home = at(m + turned * (over - m), 0)

    def finish1(h, b, rows, new):
        stage[1, h, rows] = new
        relayed = (xl == 0) & (h < RELAYED)

        @pl.when(relayed)
        def _():
            to_relay(h, b, rows).start()

        @pl.when(jnp.logical_not(relayed))
        def _():
            send(1, h, b, rows, at(after, 1)).start()

    def finish0(h, b, rows, new):
        stage[0, h, rows] = new

        @pl.when(group0_leaves)
        def _():
            send(0, h, b, rows, home).start()

        @pl.when(jnp.logical_not(group0_leaves))
        def _():
            out[rows, pl.ds(pl.multiple_of(h * HEAD_DIM, HEAD_DIM), HEAD_DIM)] = stage[0, h, rows]

    hear(1, 1)
    whole_pass(st2, 1, 1, finish1)
    hear(1, 0)
    whole_pass(st2, 1, 0, finish0)

    @pl.when(xl == 0)
    def _():
        for h, b, rows in pieces[: RELAYED * len(BLOCKS)]:
            to_relay(h, b, rows).wait_recv()
            from_relay(h, b, rows).start()

    for c in swapped + flying + ends:
        c.wait_send()
    for piece in pieces:
        send(1, *piece, at(after, 1)).wait_send()

    @pl.when(group0_leaves)
    def _():
        for piece in pieces:
            send(0, *piece, home).wait_send()

    @pl.when(xl == 0)
    def _():
        for pair in rising:
            for c in pair:
                c.wait_send()
        for piece in pieces[: RELAYED * len(BLOCKS)]:
            from_relay(*piece).wait_send()
        for piece in pieces:
            received(1, *piece)

    @pl.when((xl == 0) & (y == 0))
    def _():
        for piece in pieces:
            received(0, *piece)

    @pl.when(xl == 1)
    def _():
        for c in across:
            c.wait_send()
        for piece in pieces:
            received(0, *piece)
            received(1, *piece)


def on_device(state, key_cache, value_cache, level_gain, sigma, levels, group_len, ctx_ids, ctx_count):
    hbm = pl.BlockSpec(memory_space=pltpu.HBM)
    half = 3 * HEAD_DIM
    copies = len(SENT) + len(SECOND)
    dma = pltpu.SemaphoreType.DMA
    done = pl.pallas_call(
        kernel,
        name="queue_steps",
        out_shape=jax.ShapeDtypeStruct(state.shape[1:], jnp.bfloat16),
        in_specs=[hbm] * 9,
        out_specs=pl.BlockSpec(memory_space=pltpu.VMEM),
        scratch_shapes=[
            pltpu.VMEM((64, 32, half), jnp.bfloat16),
            pltpu.VMEM((64, 32, half), jnp.bfloat16),
            pltpu.VMEM((2, 512, half), jnp.bfloat16),
            pltpu.VMEM((2, 512, half), jnp.bfloat16),
            pltpu.VMEM((192, half), jnp.bfloat16),
            pltpu.VMEM((192, half), jnp.bfloat16),
            pltpu.VMEM((2, 512, 128), jnp.float32),
            pltpu.VMEM((2, 512, 128), jnp.float32),
            pltpu.VMEM((2, 2, 8, 8, 128), jnp.float32),
            pltpu.VMEM((6, 8, 128), jnp.int32),
            pltpu.SMEM((6, 8, 128), jnp.int32),
            pltpu.VMEM((2, 3, 512, 128), jnp.bfloat16),
            pltpu.VMEM((RELAYED, 512, 128), jnp.bfloat16),
            pltpu.VMEM(level_gain.shape, jnp.float32),
            pltpu.SMEM(sigma.shape, jnp.float32),
            pltpu.SMEM(group_len.shape, jnp.int32),
            pltpu.SMEM(levels.shape, jnp.int32),
            pltpu.SMEM(ctx_count.shape, jnp.int32),
            pltpu.SMEM(ctx_ids.shape, jnp.int32),
            dma((4,)),
            dma((6,)),
            dma((2, 6)),
            dma((2, 2, 512 // CHUNK)),
            dma((2, 2)),
            dma((copies,)),
            dma((copies,)),
            dma((2, 2, 2, 8)),
            dma((2, 2, 3, 512 // ROWS)),
            dma((2, RELAYED, 512 // ROWS)),
        ],
        compiler_params=pltpu.CompilerParams(
            collective_id=0, has_side_effects=True, vmem_limit_bytes=60 << 20
        ),
    )(state[0], key_cache[0], value_cache[0], level_gain, sigma, group_len, levels, ctx_count, ctx_ids)
    return done[None]


def solution(mesh):
    in_specs = (
        P("queue", None, "mp"),
        P("queue", None, "mp"),
        P("queue", None, "mp"),
        P(None, "mp"),
        P(),
        P("queue"),
        P(),
        P("queue", None),
        P("queue"),
    )
    return jax.shard_map(
        on_device, mesh=mesh, in_specs=in_specs, out_specs=P("queue", None, "mp"), check_vma=False
    )
```

```python
import functools
import math

import jax
import jax.numpy as jnp
from jax import lax
from jax.experimental import pallas as pl
from jax.experimental.pallas import tpu as pltpu
from jax.sharding import PartitionSpec as P

HEAD_DIM = 128
FEAT = 3072
MESH = pl.DeviceIdType.MESH
NZ, NY = 8, 4
PAIRS = NZ * NY
ROWS = 256
CHUNK = 64
EARLY, EVERY = 0, 6
LISTS_AT, TELL_AT, HEAR_AT = 6, 20, 40
RELAYED = 2


def plan():
    def onward(item):
        a, dz, dy, part = item
        if a == 0:
            if dy == 0:
                if -3 < dz <= 0:
                    yield "z+", (a, dz - 1, 0, part)
                if 0 <= dz < 3:
                    yield "z-", (a, dz + 1, 0, part)
                if dz == -2:
                    yield "z+2", (a, -4, 0, 0)
                if dz == 2:
                    yield "z-2", (a, 4, 0, 1)
                yield "y-", (a, dz, 1, part)
                yield "y+", (a, dz, -1, part)
            elif dy == 1:
                yield "y-", (a, dz, 2, part)
        else:
            if dz == 0 and dy == 0:
                yield "y-", (a, 0, 1, part)
                yield "y+", (a, 0, -1, part)
                yield "y2", (a, 0, 2, part)
            if -3 < dz <= 0 or (dz == -3 and dy in (0, 1)):
                yield "z+", (a, dz - 1, dy, part)
            if 0 <= dz < 3 or (dz == 3 and dy in (-1, 2)):
                yield "z-", (a, dz + 1, dy, part)

    held, steps = [(0, 0, 0, None), (1, 0, 0, None)], []
    while held:
        arrived = []
        for item in held:
            out = list(onward(item))
            steps.append((item, out))
            arrived.extend(got for _, got in out)
        held = arrived
    return steps


STEPS = plan()
SENT = [got for _, out in STEPS for _, got in out]
NUMBER = {got: i for i, got in enumerate(SENT)}
SECOND = {got: len(SENT) + i for i, got in enumerate(got for _, out in STEPS[:2] for _, got in out)}


def kernel(
    state, key, value, gain_in, sigma_in, lengths_in, levels_in, counts_in, lists_in,
    out,
    kbuf, vbuf, st, st2, ck, cv, inv, sq, parts, meta, meta_s, stage, relay, gain,
    sigma, lengths, level_in, count_in, ids_in,
    sem_local, sem_small, sem_meta, sem_state, sem_x, sem_send, sem_recv, sem_sq, sem_out, sem_relay,
):
    q, p = lax.axis_index("queue"), lax.axis_index("mp")
    xl, m = q % 2, q // 2
    y, z = m % NY, m // NY
    half = 3 * HEAD_DIM
    mine = pl.multiple_of(xl * half, HEAD_DIM)
    other = pl.multiple_of((1 - xl) * half, HEAD_DIM)
    me = p * 2 + xl
    after, before = (m + 1) % PAIRS, (m + PAIRS - 1) % PAIRS
    up, down = z * NY + (y + 1) % NY, z * NY + (y + NY - 1) % NY
    over, under = ((z + 1) % NZ) * NY + y, ((z + NZ - 1) % NZ) * NY + y

    def at(pair, x, mp=None):
        return {"queue": pair * 2 + x, "mp": p if mp is None else mp}

    pair_at = {
        "z+": over,
        "z-": under,
        "z+2": ((z + 2) % NZ) * NY + y,
        "z-2": ((z + NZ - 2) % NZ) * NY + y,
        "y+": up,
        "y-": down,
        "y2": z * NY + (y + 2) % NY,
    }
    to = {way: at(pair, xl) for way, pair in pair_at.items()}
    beside = {way: at(pair, 1 - xl) for way, pair in pair_at.items()}
    partner = at(m, 1 - xl)
    peers = []
    for k in range(1, 8):
        e = (me + k) % 8
        peers.append(at(m, e % 2, e // 2))

    barrier = pltpu.get_barrier_semaphore()
    greeted = [*peers, *(at(pair, x) for pair in (*pair_at.values(), after, before) for x in range(2))]
    for d in greeted:
        pl.semaphore_signal(barrier, inc=1, device_id=d, device_id_type=MESH)

    small = [
        pltpu.make_async_copy(a, b, sem_small.at[i])
        for i, (a, b) in enumerate(
            [(levels_in, level_in), (counts_in, count_in), (lists_in, ids_in),
             (sigma_in, sigma), (lengths_in, lengths), (gain_in, gain)]
        )
    ]
    for c in small:
        c.start()
    own = [
        pltpu.make_async_copy(key.at[:, pl.ds(mine, half)], kbuf.at[q], sem_local.at[0]),
        pltpu.make_async_copy(value.at[:, pl.ds(mine, half)], vbuf.at[q], sem_local.at[1]),
    ]
    for c in own:
        c.start()
    for c in small:
        c.wait()

    lane = lax.broadcasted_iota(jnp.int32, (8, 128), 1)
    tile = jnp.where(lane == 0, level_in[0, 0], jnp.where(lane == 1, count_in[0, 0], 0))
    for k in range(6):
        tile = jnp.where(lane == 2 + k, ids_in[0, k], tile)
    meta[2 + xl] = tile

    pl.semaphore_wait(barrier, len(greeted))

    def remote(src, dst, send, recv, device):
        return pltpu.make_async_remote_copy(
            src_ref=src, dst_ref=dst, send_sem=send, recv_sem=recv, device_id=device, device_id_type=MESH
        )

    swapped = [
        remote(key.at[:, pl.ds(other, half)], kbuf.at[q], sem_x.at[0, 0], sem_x.at[1, 0], partner),
        remote(value.at[:, pl.ds(other, half)], vbuf.at[q], sem_x.at[0, 1], sem_x.at[1, 1], partner),
    ]
    mine_here = meta.at[2 + xl]
    listed = [
        remote(mine_here, meta.at[row + xl], sem_meta.at[0, i], sem_meta.at[1, row + xl], d)
        for i, (row, d) in enumerate(
            [(0, at(up, 0)), (0, at(up, 1)), (2, partner), (4, at(before, 0)), (4, at(before, 1))]
        )
    ]
    def part_of(f, i):
        return state.at[pl.ds(i * CHUNK, CHUNK), f * half : (f + 1) * half]

    chunks = range(512 // CHUNK)
    rising = [
        [remote(part_of(f, i), st.at[0, pl.ds(i * CHUNK, CHUNK)], sem_state.at[0, f, i], sem_state.at[1, 0, i], at(up, f)) for f in range(2)]
        for i in chunks
    ]
    across = [
        remote(part_of(0, i), st.at[1, pl.ds(i * CHUNK, CHUNK)], sem_state.at[0, 0, i], sem_state.at[1, 1, i], partner)
        for i in chunks
    ]
    staying = pltpu.make_async_copy(state.at[:, half:], st.at[1], sem_local.at[3])

    def move(i):
        @pl.when(xl == 0)
        def _():
            for c in rising[i]:
                c.start()

    def region(item):
        a, dz, dy, part = item
        buf = vbuf if a else kbuf
        pair = ((z + dz + NZ) % NZ) * NY + (y + dy + NY) % NY
        return buf.at[pl.ds(pair * 2, 2)] if part is None else buf.at[pl.ds(pair * 2 + part, 1)]

    bufs, flying = (kbuf, vbuf), []
    theirs = 2 * m + 1 - xl
    for c in listed:
        c.start()
    for (item, out_items), source in zip(STEPS[:2], (key, value)):
        for way, got in out_items:
            for side, numbers, device in ((mine, NUMBER, to[way]), (other, SECOND, beside[way])):
                c = remote(
                    source.at[:, pl.ds(side, half)], bufs[item[0]].at[q],
                    sem_send.at[numbers[got]], sem_recv.at[numbers[got]], device,
                )
                c.start()
                flying.append(c)
    for c in swapped:
        c.start()

    @pl.when(xl == 1)
    def _():
        staying.start()
        for c in across:
            c.start()

    for c in own:
        c.wait()
    for i, buf in enumerate(bufs):
        remote(buf.at[theirs], buf.at[theirs], sem_x.at[0, i], sem_x.at[1, i], partner).wait_recv()

    def landed(j):
        for i in chunks:
            here = st.at[j, pl.ds(i * CHUNK, CHUNK)]
            remote(here, here, sem_state.at[0, 0, i], sem_state.at[1, j, i], partner).wait_recv()

    def squares(j):
        @pl.loop(0, 4)
        def _(b):
            rows = pl.ds(b * 128, 128)
            x = st[j, rows, :].astype(jnp.float32)
            x = x * x
            sq[j, rows, :] = x[:, :128] + x[:, 128:256] + x[:, 256:]

    row8 = lax.broadcasted_iota(jnp.int32, (8, 128), 0)
    ends = []

    def tell(step, j):
        mine8 = jnp.zeros((8, 128), jnp.float32)
        for r in range(4):
            piece = sq[j, r * 128 : (r + 1) * 128, :]
            line = jnp.sum(jnp.transpose(piece), axis=0, keepdims=True)
            mine8 = jnp.where(row8 == r, jnp.broadcast_to(line, (8, 128)), mine8)
        parts[step, j, me] = mine8
        for k in range(1, 8):
            c = remote(
                parts.at[step, j, me], parts.at[step, j, me],
                sem_sq.at[0, step, j, k], sem_sq.at[1, step, j, k], peers[k - 1],
            )
            c.start()
            ends.append(c)

    def hear(step, j):
        for k in range(1, 8):
            e = (me + 8 - k) % 8
            remote(
                parts.at[step, j, e], parts.at[step, j, e],
                sem_sq.at[0, step, j, k], sem_sq.at[1, step, j, k], peers[k - 1],
            ).wait_recv()
        whole = parts[step, j, 0]
        for e in range(1, 8):
            whole = whole + parts[step, j, e]
        factor = lax.rsqrt(whole / FEAT + 1e-06)
        for r in range(4):
            wide = jnp.broadcast_to(factor[r : r + 1, :], (128, 128))
            inv[j, r * 128 : (r + 1) * 128, :] = jnp.transpose(wide)

    def read_lists():
        for row in (0, 1, 3 - xl, 4, 5):
            remote(meta.at[row], meta.at[row], sem_meta.at[0, 0], sem_meta.at[1, row], partner).wait_recv()
        for c in listed:
            c.wait_send()
        into_s = pltpu.make_async_copy(meta, meta_s, sem_local.at[2])
        into_s.start()
        into_s.wait()

    waiting = list(chunks)
    last = max(i for i, (_, out_items) in enumerate(STEPS) if out_items)

    def arrived(item):
        if item in NUMBER:
            n = NUMBER[item]
            here = region(item)
            if item in SECOND:
                for slot, n in ((xl, n), (1 - xl, SECOND[item])):
                    one = here.at[pl.ds(slot, 1)]
                    remote(one, one, sem_send.at[n], sem_recv.at[n], to["y+"]).wait_recv()
            else:
                remote(here, here, sem_send.at[n], sem_recv.at[n], to["y+"]).wait_recv()

    for i, (item, out_items) in enumerate(STEPS[: last + 1]):
        arrived(item)
        for way, got in out_items if i > 1 else ():
            n = NUMBER[got]
            src = region((item[0], item[1], item[2], got[3]))
            c = remote(src, src, sem_send.at[n], sem_recv.at[n], to[way])
            c.start()
            flying.append(c)
        if i == LISTS_AT:
            read_lists()
        if i == TELL_AT:
            pl.when(xl == 0)(functools.partial(landed, 1))
            pl.when(xl == 1)(staying.wait)
            squares(1)
            tell(0, 1)
        if i == HEAR_AT:
            hear(0, 1)
        if waiting and i >= EARLY and (i - EARLY) % EVERY == 0:
            move(waiting.pop(0))
    for i in waiting:
        move(i)

    scale = HEAD_DIM ** (-0.5) * math.log2(math.e)
    nt = (((1,), (1,)), ((), ()))

    def fetch(step, j):
        for k in range(6):
            block = meta_s[3 * j + step, 0, 2 + k]
            ck[k * 32 : (k + 1) * 32, :] = kbuf[block]
            cv[k * 32 : (k + 1) * 32, :] = vbuf[block]

    def at_head(source, step, j, h):
        level = meta_s[3 * j + step, 0, 0]
        length = lengths[2 * m + 1 if j else 2 * down]
        columns = pl.ds(pl.multiple_of(h * HEAD_DIM, HEAD_DIM), HEAD_DIM)
        table = gain[:, pl.ds(pl.multiple_of(mine + h * HEAD_DIM, HEAD_DIM), HEAD_DIM)]
        level_row = lax.broadcasted_iota(jnp.int32, table.shape, 0)
        gains = jnp.sum(jnp.where(level_row == level, table, 0.0), axis=0, keepdims=True)
        keys = (source[j, :, columns].astype(jnp.float32) * inv[j]).astype(jnp.bfloat16)
        return columns, keys, gains, length

    def own_scores(source, j, rows, columns, keys, gains, length):
        x = source[j, rows, columns].astype(jnp.float32)
        queries = (x * inv[j, rows, :] * gains).astype(jnp.bfloat16)
        lane = lax.broadcasted_iota(jnp.int32, (1, 256), 1) + 256
        bias = jnp.where(lane < length, 0.0, -jnp.inf)
        s0 = lax.dot_general(queries, keys[:256], nt, preferred_element_type=jnp.float32)
        s1 = lax.dot_general(queries, keys[256:], nt, preferred_element_type=jnp.float32) + bias
        return queries, s0, s1

    def more_scores(queries, step, j, columns):
        lane = lax.broadcasted_iota(jnp.int32, (1, 192), 1)
        bias = jnp.where(lane < meta_s[3 * j + step, 0, 1] * 32, 0.0, -jnp.inf)
        return lax.dot_general(queries, ck[:, columns], nt, preferred_element_type=jnp.float32) + bias

    def highest(*scores):
        tops = [jnp.max(a, axis=1, keepdims=True) for a in scores]
        return functools.reduce(jnp.maximum, tops)

    def weighted(top, *terms):
        total, o = 0.0, 0.0
        for a, values in terms:
            w = jnp.exp2((a - top) * scale)
            total = total + jnp.sum(w, axis=1, keepdims=True)
            o = o + jnp.dot(w.astype(jnp.bfloat16), values, preferred_element_type=jnp.float32)
        return total, o

    def advanced(source, step, j, b, rows, columns, length, total, o):
        level = meta_s[3 * j + step, 0, 0]
        size = sigma[level + 1] - sigma[level]
        x = source[j, rows, columns].astype(jnp.float32)
        live = lax.broadcasted_iota(jnp.int32, (ROWS, 1), 0) + b * ROWS < length
        return jnp.where(live, x + size * (o * (1.0 / total)), x).astype(jnp.bfloat16)

    BLOCKS = [(b, slice(b * ROWS, (b + 1) * ROWS)) for b in range(512 // ROWS)]

    def whole_pass(source, step, j, finish, after_head=lambda h: None):
        def one(h):
            columns, keys, gains, length = at_head(source, step, j, h)
            scored = []
            for b, rows in BLOCKS:
                queries, s0, s1 = own_scores(source, j, rows, columns, keys, gains, length)
                scored.append((s0, s1, more_scores(queries, step, j, columns)))
            peaks = [highest(*a) for a in scored]
            values = source[j, :256, columns], source[j, 256:, columns], cv[:, columns]
            summed = [weighted(top, *zip(a, values)) for top, a in zip(peaks, scored)]
            for (b, rows), (total, o) in zip(BLOCKS, summed):
                finish(h, b, rows, advanced(source, step, j, b, rows, columns, length, total, o))

        for h in range(3):
            one(h)
            after_head(h)

    landed(0)
    squares(0)
    tell(0, 0)
    for item, _ in STEPS[last + 1 :]:
        arrived(item)
    def keep(j):
        def finish(h, b, rows, new):
            columns = pl.ds(pl.multiple_of(h * HEAD_DIM, HEAD_DIM), HEAD_DIM)
            st2[j, rows, columns] = new
            wide = new.astype(jnp.float32)
            sq[j, rows, :] = wide * wide if h == 0 else sq[j, rows, :] + wide * wide

        return finish

    for j in (1, 0):
        fetch(0, j)
        if j == 0:
            hear(0, 0)
        whole_pass(st, 0, j, keep(j))
        tell(1, j)

    def place(f, h, rows):
        return out.at[rows, pl.ds(pl.multiple_of(f * half + h * HEAD_DIM, HEAD_DIM), HEAD_DIM)]

    def send(j, h, b, rows, device):
        return remote(stage.at[j, h, rows], place(xl, h, rows), sem_out.at[0, j, h, b], sem_out.at[1, xl, h, b], device)

    def to_relay(h, b, rows):
        return remote(stage.at[1, h, rows], relay.at[h, rows], sem_out.at[0, 1, h, b], sem_relay.at[1, h, b], at(after, 0))

    def from_relay(h, b, rows):
        return remote(relay.at[h, rows], place(0, h, rows), sem_relay.at[0, h, b], sem_out.at[1, 0, h, b], partner)

    def received(f, h, b, rows):
        here = place(f, h, rows)
        remote(stage.at[0, h, rows], here, sem_out.at[0, 0, h, b], sem_out.at[1, f, h, b], partner).wait_recv()

    pieces = [(h, b, rows) for h in range(3) for b, rows in BLOCKS]

    turned = (y == 0).astype(jnp.int32)
    group0_leaves = (xl == 1) | (y == 0)
    home = at(m + turned * (over - m), 0)

    def keep1(h, b, rows, new):
        stage[1, h, rows] = new

    def send1(h):
        def onward():
            for b, rows in BLOCKS:
                send(1, h, b, rows, at(after, 1)).start()

        def relayed():
            for b, rows in BLOCKS:
                to_relay(h, b, rows).start()

        if h < RELAYED:
            pl.when(xl == 0)(relayed)
            pl.when(xl == 1)(onward)
        else:
            onward()

    def keep0(h, b, rows, new):
        stage[0, h, rows] = new

    def send0(h):
        @pl.when(group0_leaves)
        def _():
            for b, rows in BLOCKS:
                send(0, h, b, rows, home).start()

        @pl.when(jnp.logical_not(group0_leaves))
        def _():
            out[:, h * HEAD_DIM : (h + 1) * HEAD_DIM] = stage[0, h]

    fetch(1, 1)
    hear(1, 1)
    whole_pass(st2, 1, 1, keep1, send1)
    fetch(1, 0)
    hear(1, 0)
    whole_pass(st2, 1, 0, keep0, send0)

    @pl.when(xl == 0)
    def _():
        for h, b, rows in pieces[: RELAYED * len(BLOCKS)]:
            to_relay(h, b, rows).wait_recv()
            from_relay(h, b, rows).start()

    for c in swapped + flying + ends:
        c.wait_send()
    for piece in pieces:
        send(1, *piece, at(after, 1)).wait_send()

    @pl.when(group0_leaves)
    def _():
        for piece in pieces:
            send(0, *piece, home).wait_send()

    @pl.when(xl == 0)
    def _():
        for pair in rising:
            for c in pair:
                c.wait_send()
        for piece in pieces[: RELAYED * len(BLOCKS)]:
            from_relay(*piece).wait_send()
        for piece in pieces:
            received(1, *piece)

    @pl.when((xl == 0) & (y == 0))
    def _():
        for piece in pieces:
            received(0, *piece)

    @pl.when(xl == 1)
    def _():
        for c in across:
            c.wait_send()
        for piece in pieces:
            received(0, *piece)
            received(1, *piece)


def on_device(state, key_cache, value_cache, level_gain, sigma, levels, group_len, ctx_ids, ctx_count):
    hbm = pl.BlockSpec(memory_space=pltpu.HBM)
    half = 3 * HEAD_DIM
    copies = len(SENT) + len(SECOND)
    dma = pltpu.SemaphoreType.DMA
    done = pl.pallas_call(
        kernel,
        name="queue_steps",
        out_shape=jax.ShapeDtypeStruct(state.shape[1:], jnp.bfloat16),
        in_specs=[hbm] * 9,
        out_specs=pl.BlockSpec(memory_space=pltpu.VMEM),
        scratch_shapes=[
            pltpu.VMEM((64, 32, half), jnp.bfloat16),
            pltpu.VMEM((64, 32, half), jnp.bfloat16),
            pltpu.VMEM((2, 512, half), jnp.bfloat16),
            pltpu.VMEM((2, 512, half), jnp.bfloat16),
            pltpu.VMEM((192, half), jnp.bfloat16),
            pltpu.VMEM((192, half), jnp.bfloat16),
            pltpu.VMEM((2, 512, 128), jnp.float32),
            pltpu.VMEM((2, 512, 128), jnp.float32),
            pltpu.VMEM((2, 2, 8, 8, 128), jnp.float32),
            pltpu.VMEM((6, 8, 128), jnp.int32),
            pltpu.SMEM((6, 8, 128), jnp.int32),
            pltpu.VMEM((2, 3, 512, 128), jnp.bfloat16),
            pltpu.VMEM((RELAYED, 512, 128), jnp.bfloat16),
            pltpu.VMEM(level_gain.shape, jnp.float32),
            pltpu.SMEM(sigma.shape, jnp.float32),
            pltpu.SMEM(group_len.shape, jnp.int32),
            pltpu.SMEM((1, 1), jnp.int32),
            pltpu.SMEM((1, 1), jnp.int32),
            pltpu.SMEM(ctx_ids.shape, jnp.int32),
            dma((4,)),
            dma((6,)),
            dma((2, 6)),
            dma((2, 2, 512 // CHUNK)),
            dma((2, 2)),
            dma((copies,)),
            dma((copies,)),
            dma((2, 2, 2, 8)),
            dma((2, 2, 3, 512 // ROWS)),
            dma((2, RELAYED, 512 // ROWS)),
        ],
        compiler_params=pltpu.CompilerParams(
            collective_id=0, has_side_effects=True, vmem_limit_bytes=60 << 20
        ),
    )(state[0], key_cache[0], value_cache[0], level_gain, sigma, group_len, levels[None], ctx_count[None], ctx_ids)
    return done[None]


def solution(mesh):
    in_specs = (
        P("queue", None, "mp"),
        P("queue", None, "mp"),
        P("queue", None, "mp"),
        P(None, "mp"),
        P(),
        P("queue"),
        P(),
        P("queue", None),
        P("queue"),
    )
    return jax.shard_map(
        on_device, mesh=mesh, in_specs=in_specs, out_specs=P("queue", None, "mp"), check_vma=False
    )
```

```python
import functools
import math

import jax
import jax.numpy as jnp
from jax import lax
from jax.experimental import pallas as pl
from jax.experimental.pallas import tpu as pltpu
from jax.sharding import PartitionSpec as P

HEAD_DIM = 128
FEAT = 3072
MESH = pl.DeviceIdType.MESH
NZ, NY = 8, 4
PAIRS = NZ * NY
ROWS = 256
CHUNK = 64
EARLY, EVERY = 0, 6
LISTS_AT, TELL_AT, HEAR_AT = 30, 24, 58
RELAYED = 2


def plan():
    def onward(item):
        a, dz, dy, part = item
        if a == 0:
            if dy == 0:
                if -3 < dz <= 0:
                    yield "z+", (a, dz - 1, 0, part)
                if 0 <= dz < 3:
                    yield "z-", (a, dz + 1, 0, part)
                if dz == -2:
                    yield "z+2", (a, -4, 0, 0)
                if dz == 2:
                    yield "z-2", (a, 4, 0, 1)
                yield "y-", (a, dz, 1, part)
                yield "y+", (a, dz, -1, part)
            elif dy == 1:
                yield "y-", (a, dz, 2, part)
        else:
            if dz == 0 and dy == 0:
                yield "y-", (a, 0, 1, part)
                yield "y+", (a, 0, -1, part)
                yield "y2", (a, 0, 2, part)
            if -3 < dz <= 0 or (dz == -3 and dy in (0, 1)):
                yield "z+", (a, dz - 1, dy, part)
            if 0 <= dz < 3 or (dz == 3 and dy in (-1, 2)):
                yield "z-", (a, dz + 1, dy, part)

    held, steps = [(0, 0, 0, None), (1, 0, 0, None)], []
    while held:
        arrived = []
        for item in held:
            out = list(onward(item))
            steps.append((item, out))
            arrived.extend(got for _, got in out)
        held = arrived
    return steps


STEPS = plan()
SENT = [got for _, out in STEPS for _, got in out]
NUMBER = {got: i for i, got in enumerate(SENT)}
SECOND = {got: len(SENT) + i for i, got in enumerate(got for _, out in STEPS[:2] for _, got in out)}


def kernel(
    state, key, value, gain_in, sigma_in, lengths_in, levels_in, counts_in, lists_in,
    out,
    kbuf, vbuf, st, st2, ck, cv, inv, sq, parts, meta, meta_s, stage, relay, gain,
    sigma, lengths, level_in, count_in, ids_in,
    sem_local, sem_small, sem_meta, sem_state, sem_x, sem_send, sem_recv, sem_sq, sem_out, sem_relay,
):
    q, p = lax.axis_index("queue"), lax.axis_index("mp")
    xl, m = q % 2, q // 2
    y, z = m % NY, m // NY
    half = 3 * HEAD_DIM
    mine = pl.multiple_of(xl * half, HEAD_DIM)
    other = pl.multiple_of((1 - xl) * half, HEAD_DIM)
    me = p * 2 + xl
    after, before = (m + 1) % PAIRS, (m + PAIRS - 1) % PAIRS
    up, down = z * NY + (y + 1) % NY, z * NY + (y + NY - 1) % NY
    over, under = ((z + 1) % NZ) * NY + y, ((z + NZ - 1) % NZ) * NY + y

    def at(pair, x, mp=None):
        return {"queue": pair * 2 + x, "mp": p if mp is None else mp}

    pair_at = {
        "z+": over,
        "z-": under,
        "z+2": ((z + 2) % NZ) * NY + y,
        "z-2": ((z + NZ - 2) % NZ) * NY + y,
        "y+": up,
        "y-": down,
        "y2": z * NY + (y + 2) % NY,
    }
    to = {way: at(pair, xl) for way, pair in pair_at.items()}
    beside = {way: at(pair, 1 - xl) for way, pair in pair_at.items()}
    partner = at(m, 1 - xl)
    peers = []
    for k in range(1, 8):
        e = (me + k) % 8
        peers.append(at(m, e % 2, e // 2))

    barrier = pltpu.get_barrier_semaphore()
    greeted = [*peers, *(at(pair, x) for pair in (*pair_at.values(), after, before) for x in range(2))]
    for d in greeted:
        pl.semaphore_signal(barrier, inc=1, device_id=d, device_id_type=MESH)

    small = [
        pltpu.make_async_copy(a, b, sem_small.at[i])
        for i, (a, b) in enumerate(
            [(levels_in, level_in), (counts_in, count_in), (lists_in, ids_in),
             (sigma_in, sigma), (lengths_in, lengths), (gain_in, gain)]
        )
    ]
    for c in small:
        c.start()
    own = [
        pltpu.make_async_copy(key.at[:, pl.ds(mine, half)], kbuf.at[q], sem_local.at[0]),
        pltpu.make_async_copy(value.at[:, pl.ds(mine, half)], vbuf.at[q], sem_local.at[1]),
    ]
    for c in own:
        c.start()
    for c in small:
        c.wait()

    lane = lax.broadcasted_iota(jnp.int32, (8, 128), 1)
    tile = jnp.where(lane == 0, level_in[0, 0], jnp.where(lane == 1, count_in[0, 0], 0))
    for k in range(6):
        tile = jnp.where(lane == 2 + k, ids_in[0, k], tile)
    meta[2 + xl] = tile

    pl.semaphore_wait(barrier, len(greeted))

    def remote(src, dst, send, recv, device):
        return pltpu.make_async_remote_copy(
            src_ref=src, dst_ref=dst, send_sem=send, recv_sem=recv, device_id=device, device_id_type=MESH
        )

    swapped = [
        remote(key.at[:, pl.ds(other, half)], kbuf.at[q], sem_x.at[0, 0], sem_x.at[1, 0], partner),
        remote(value.at[:, pl.ds(other, half)], vbuf.at[q], sem_x.at[0, 1], sem_x.at[1, 1], partner),
    ]
    mine_here = meta.at[2 + xl]
    listed = [
        remote(mine_here, meta.at[row + xl], sem_meta.at[0, i], sem_meta.at[1, row + xl], d)
        for i, (row, d) in enumerate(
            [(0, at(up, 0)), (0, at(up, 1)), (2, partner), (4, at(before, 0)), (4, at(before, 1))]
        )
    ]
    def part_of(f, i):
        return state.at[pl.ds(i * CHUNK, CHUNK), f * half : (f + 1) * half]

    chunks = range(512 // CHUNK)
    rising = [
        [remote(part_of(f, i), st.at[0, pl.ds(i * CHUNK, CHUNK)], sem_state.at[0, f, i], sem_state.at[1, 0, i], at(up, f)) for f in range(2)]
        for i in chunks
    ]
    across = [
        remote(part_of(0, i), st.at[1, pl.ds(i * CHUNK, CHUNK)], sem_state.at[0, 0, i], sem_state.at[1, 1, i], partner)
        for i in chunks
    ]
    staying = pltpu.make_async_copy(state.at[:, half:], st.at[1], sem_local.at[3])

    def move(i):
        @pl.when(xl == 0)
        def _():
            for c in rising[i]:
                c.start()

    def region(item):
        a, dz, dy, part = item
        buf = vbuf if a else kbuf
        pair = ((z + dz + NZ) % NZ) * NY + (y + dy + NY) % NY
        return buf.at[pl.ds(pair * 2, 2)] if part is None else buf.at[pl.ds(pair * 2 + part, 1)]

    bufs, flying = (kbuf, vbuf), []
    theirs = 2 * m + 1 - xl
    for c in listed:
        c.start()
    for (item, out_items), source in zip(STEPS[:2], (key, value)):
        for way, got in out_items:
            for side, numbers, device in ((mine, NUMBER, to[way]), (other, SECOND, beside[way])):
                c = remote(
                    source.at[:, pl.ds(side, half)], bufs[item[0]].at[q],
                    sem_send.at[numbers[got]], sem_recv.at[numbers[got]], device,
                )
                c.start()
                flying.append(c)
    for c in swapped:
        c.start()

    @pl.when(xl == 1)
    def _():
        staying.start()
        for c in across:
            c.start()


    def landed(j):
        for i in chunks:
            here = st.at[j, pl.ds(i * CHUNK, CHUNK)]
            remote(here, here, sem_state.at[0, 0, i], sem_state.at[1, j, i], partner).wait_recv()

    def squares(j):
        @pl.loop(0, 4)
        def _(b):
            rows = pl.ds(b * 128, 128)
            x = st[j, rows, :].astype(jnp.float32)
            x = x * x
            sq[j, rows, :] = x[:, :128] + x[:, 128:256] + x[:, 256:]

    row8 = lax.broadcasted_iota(jnp.int32, (8, 128), 0)
    ends = []

    def tell(step, j):
        mine8 = jnp.zeros((8, 128), jnp.float32)
        for r in range(4):
            piece = sq[j, r * 128 : (r + 1) * 128, :]
            line = jnp.sum(jnp.transpose(piece), axis=0, keepdims=True)
            mine8 = jnp.where(row8 == r, jnp.broadcast_to(line, (8, 128)), mine8)
        parts[step, j, me] = mine8
        for k in range(1, 8):
            c = remote(
                parts.at[step, j, me], parts.at[step, j, me],
                sem_sq.at[0, step, j, k], sem_sq.at[1, step, j, k], peers[k - 1],
            )
            c.start()
            ends.append(c)

    def hear(step, j):
        for k in range(1, 8):
            e = (me + 8 - k) % 8
            remote(
                parts.at[step, j, e], parts.at[step, j, e],
                sem_sq.at[0, step, j, k], sem_sq.at[1, step, j, k], peers[k - 1],
            ).wait_recv()
        whole = parts[step, j, 0]
        for e in range(1, 8):
            whole = whole + parts[step, j, e]
        factor = lax.rsqrt(whole / FEAT + 1e-06)
        for r in range(4):
            wide = jnp.broadcast_to(factor[r : r + 1, :], (128, 128))
            inv[j, r * 128 : (r + 1) * 128, :] = jnp.transpose(wide)

    def read_lists():
        for row in (0, 1, 3 - xl, 4, 5):
            remote(meta.at[row], meta.at[row], sem_meta.at[0, 0], sem_meta.at[1, row], partner).wait_recv()
        for c in listed:
            c.wait_send()
        into_s = pltpu.make_async_copy(meta, meta_s, sem_local.at[2])
        into_s.start()
        into_s.wait()

    waiting = list(chunks)
    last = max(i for i, (_, out_items) in enumerate(STEPS) if out_items)

    def arrived(item):
        if item in NUMBER:
            n = NUMBER[item]
            here = region(item)
            if item in SECOND:
                for slot, n in ((xl, n), (1 - xl, SECOND[item])):
                    one = here.at[pl.ds(slot, 1)]
                    remote(one, one, sem_send.at[n], sem_recv.at[n], to["y+"]).wait_recv()
            else:
                remote(here, here, sem_send.at[n], sem_recv.at[n], to["y+"]).wait_recv()

    for i, (item, out_items) in enumerate(STEPS[: last + 1]):
        arrived(item)
        for way, got in out_items if i > 1 else ():
            n = NUMBER[got]
            src = region((item[0], item[1], item[2], got[3]))
            c = remote(src, src, sem_send.at[n], sem_recv.at[n], to[way])
            c.start()
            flying.append(c)
        if i == LISTS_AT:
            read_lists()
        if i == TELL_AT:
            pl.when(xl == 0)(functools.partial(landed, 1))
            pl.when(xl == 1)(staying.wait)
            squares(1)
            tell(0, 1)
        if i == HEAR_AT:
            hear(0, 1)
        if waiting and i >= EARLY and (i - EARLY) % EVERY == 0:
            move(waiting.pop(0))
    for i in waiting:
        move(i)

    scale = HEAD_DIM ** (-0.5) * math.log2(math.e)
    nt = (((1,), (1,)), ((), ()))

    def fetch(step, j):
        for k in range(6):
            block = meta_s[3 * j + step, 0, 2 + k]
            ck[k * 32 : (k + 1) * 32, :] = kbuf[block]
            cv[k * 32 : (k + 1) * 32, :] = vbuf[block]

    def at_head(source, step, j, h):
        level = meta_s[3 * j + step, 0, 0]
        length = lengths[2 * m + 1 if j else 2 * down]
        columns = pl.ds(pl.multiple_of(h * HEAD_DIM, HEAD_DIM), HEAD_DIM)
        table = gain[:, pl.ds(pl.multiple_of(mine + h * HEAD_DIM, HEAD_DIM), HEAD_DIM)]
        level_row = lax.broadcasted_iota(jnp.int32, table.shape, 0)
        gains = jnp.sum(jnp.where(level_row == level, table, 0.0), axis=0, keepdims=True)
        keys = (source[j, :, columns].astype(jnp.float32) * inv[j]).astype(jnp.bfloat16)
        return columns, keys, gains, length

    def own_scores(source, j, rows, columns, keys, gains, length):
        x = source[j, rows, columns].astype(jnp.float32)
        queries = (x * inv[j, rows, :] * gains).astype(jnp.bfloat16)
        lane = lax.broadcasted_iota(jnp.int32, (1, 256), 1) + 256
        bias = jnp.where(lane < length, 0.0, -jnp.inf)
        s0 = lax.dot_general(queries, keys[:256], nt, preferred_element_type=jnp.float32)
        s1 = lax.dot_general(queries, keys[256:], nt, preferred_element_type=jnp.float32) + bias
        return queries, s0, s1

    def more_scores(queries, step, j, columns):
        lane = lax.broadcasted_iota(jnp.int32, (1, 192), 1)
        bias = jnp.where(lane < meta_s[3 * j + step, 0, 1] * 32, 0.0, -jnp.inf)
        return lax.dot_general(queries, ck[:, columns], nt, preferred_element_type=jnp.float32) + bias

    def highest(*scores):
        tops = [jnp.max(a, axis=1, keepdims=True) for a in scores]
        return functools.reduce(jnp.maximum, tops)

    def weighted(top, *terms):
        total, o = 0.0, 0.0
        for a, values in terms:
            w = jnp.exp2((a - top) * scale)
            total = total + jnp.sum(w, axis=1, keepdims=True)
            o = o + jnp.dot(w.astype(jnp.bfloat16), values, preferred_element_type=jnp.float32)
        return total, o

    def advanced(source, step, j, b, rows, columns, length, total, o):
        level = meta_s[3 * j + step, 0, 0]
        size = sigma[level + 1] - sigma[level]
        x = source[j, rows, columns].astype(jnp.float32)
        live = lax.broadcasted_iota(jnp.int32, (ROWS, 1), 0) + b * ROWS < length
        return jnp.where(live, x + size * (o * (1.0 / total)), x).astype(jnp.bfloat16)

    BLOCKS = [(b, slice(b * ROWS, (b + 1) * ROWS)) for b in range(512 // ROWS)]

    def whole_pass(source, step, j, finish, after_head=lambda h: None):
        def one(h):
            columns, keys, gains, length = at_head(source, step, j, h)
            scored = []
            for b, rows in BLOCKS:
                queries, s0, s1 = own_scores(source, j, rows, columns, keys, gains, length)
                scored.append((s0, s1, more_scores(queries, step, j, columns)))
            peaks = [highest(*a) for a in scored]
            values = source[j, :256, columns], source[j, 256:, columns], cv[:, columns]
            summed = [weighted(top, *zip(a, values)) for top, a in zip(peaks, scored)]
            for (b, rows), (total, o) in zip(BLOCKS, summed):
                finish(h, b, rows, advanced(source, step, j, b, rows, columns, length, total, o))

        for h in range(3):
            one(h)
            after_head(h)

    for c in own:
        c.wait()
    for i, buf in enumerate(bufs):
        remote(buf.at[theirs], buf.at[theirs], sem_x.at[0, i], sem_x.at[1, i], partner).wait_recv()
    landed(0)
    squares(0)
    tell(0, 0)
    for item, _ in STEPS[last + 1 :]:
        arrived(item)
    def keep(j):
        def finish(h, b, rows, new):
            columns = pl.ds(pl.multiple_of(h * HEAD_DIM, HEAD_DIM), HEAD_DIM)
            st2[j, rows, columns] = new
            wide = new.astype(jnp.float32)
            sq[j, rows, :] = wide * wide if h == 0 else sq[j, rows, :] + wide * wide

        return finish

    for j in (1, 0):
        fetch(0, j)
        if j == 0:
            hear(0, 0)
        whole_pass(st, 0, j, keep(j))
        tell(1, j)

    def place(f, h, rows):
        return out.at[rows, pl.ds(pl.multiple_of(f * half + h * HEAD_DIM, HEAD_DIM), HEAD_DIM)]

    def send(j, h, b, rows, device):
        return remote(stage.at[j, h, rows], place(xl, h, rows), sem_out.at[0, j, h, b], sem_out.at[1, xl, h, b], device)

    def to_relay(h, b, rows):
        return remote(stage.at[1, h, rows], relay.at[h, rows], sem_out.at[0, 1, h, b], sem_relay.at[1, h, b], at(after, 0))

    def from_relay(h, b, rows):
        return remote(relay.at[h, rows], place(0, h, rows), sem_relay.at[0, h, b], sem_out.at[1, 0, h, b], partner)

    def received(f, h, b, rows):
        here = place(f, h, rows)
        remote(stage.at[0, h, rows], here, sem_out.at[0, 0, h, b], sem_out.at[1, f, h, b], partner).wait_recv()

    pieces = [(h, b, rows) for h in range(3) for b, rows in BLOCKS]

    turned = (y == 0).astype(jnp.int32)
    group0_leaves = (xl == 1) | (y == 0)
    home = at(m + turned * (over - m), 0)

    def keep1(h, b, rows, new):
        stage[1, h, rows] = new

    def send1(h):
        def onward():
            for b, rows in BLOCKS:
                send(1, h, b, rows, at(after, 1)).start()

        def relayed():
            for b, rows in BLOCKS:
                to_relay(h, b, rows).start()

        if h < RELAYED:
            pl.when(xl == 0)(relayed)
            pl.when(xl == 1)(onward)
        else:
            onward()

    def keep0(h, b, rows, new):
        stage[0, h, rows] = new

    def send0(h):
        @pl.when(group0_leaves)
        def _():
            for b, rows in BLOCKS:
                send(0, h, b, rows, home).start()

        @pl.when(jnp.logical_not(group0_leaves))
        def _():
            out[:, h * HEAD_DIM : (h + 1) * HEAD_DIM] = stage[0, h]

    fetch(1, 1)
    hear(1, 1)
    whole_pass(st2, 1, 1, keep1, send1)
    fetch(1, 0)
    hear(1, 0)
    whole_pass(st2, 1, 0, keep0, send0)

    @pl.when(xl == 0)
    def _():
        for h, b, rows in pieces[: RELAYED * len(BLOCKS)]:
            to_relay(h, b, rows).wait_recv()
            from_relay(h, b, rows).start()

    for c in swapped + flying + ends:
        c.wait_send()
    for piece in pieces:
        send(1, *piece, at(after, 1)).wait_send()

    @pl.when(group0_leaves)
    def _():
        for piece in pieces:
            send(0, *piece, home).wait_send()

    @pl.when(xl == 0)
    def _():
        for pair in rising:
            for c in pair:
                c.wait_send()
        for piece in pieces[: RELAYED * len(BLOCKS)]:
            from_relay(*piece).wait_send()
        for piece in pieces:
            received(1, *piece)

    @pl.when((xl == 0) & (y == 0))
    def _():
        for piece in pieces:
            received(0, *piece)

    @pl.when(xl == 1)
    def _():
        for c in across:
            c.wait_send()
        for piece in pieces:
            received(0, *piece)
            received(1, *piece)


def on_device(state, key_cache, value_cache, level_gain, sigma, levels, group_len, ctx_ids, ctx_count):
    hbm = pl.BlockSpec(memory_space=pltpu.HBM)
    half = 3 * HEAD_DIM
    copies = len(SENT) + len(SECOND)
    dma = pltpu.SemaphoreType.DMA
    done = pl.pallas_call(
        kernel,
        name="queue_steps",
        out_shape=jax.ShapeDtypeStruct(state.shape[1:], jnp.bfloat16),
        in_specs=[hbm] * 9,
        out_specs=pl.BlockSpec(memory_space=pltpu.VMEM),
        scratch_shapes=[
            pltpu.VMEM((64, 32, half), jnp.bfloat16),
            pltpu.VMEM((64, 32, half), jnp.bfloat16),
            pltpu.VMEM((2, 512, half), jnp.bfloat16),
            pltpu.VMEM((2, 512, half), jnp.bfloat16),
            pltpu.VMEM((192, half), jnp.bfloat16),
            pltpu.VMEM((192, half), jnp.bfloat16),
            pltpu.VMEM((2, 512, 128), jnp.float32),
            pltpu.VMEM((2, 512, 128), jnp.float32),
            pltpu.VMEM((2, 2, 8, 8, 128), jnp.float32),
            pltpu.VMEM((6, 8, 128), jnp.int32),
            pltpu.SMEM((6, 8, 128), jnp.int32),
            pltpu.VMEM((2, 3, 512, 128), jnp.bfloat16),
            pltpu.VMEM((RELAYED, 512, 128), jnp.bfloat16),
            pltpu.VMEM(level_gain.shape, jnp.float32),
            pltpu.SMEM(sigma.shape, jnp.float32),
            pltpu.SMEM(group_len.shape, jnp.int32),
            pltpu.SMEM((1, 1), jnp.int32),
            pltpu.SMEM((1, 1), jnp.int32),
            pltpu.SMEM(ctx_ids.shape, jnp.int32),
            dma((4,)),
            dma((6,)),
            dma((2, 6)),
            dma((2, 2, 512 // CHUNK)),
            dma((2, 2)),
            dma((copies,)),
            dma((copies,)),
            dma((2, 2, 2, 8)),
            dma((2, 2, 3, 512 // ROWS)),
            dma((2, RELAYED, 512 // ROWS)),
        ],
        compiler_params=pltpu.CompilerParams(
            collective_id=0, has_side_effects=True, vmem_limit_bytes=60 << 20
        ),
    )(state[0], key_cache[0], value_cache[0], level_gain, sigma, group_len, levels[None], ctx_count[None], ctx_ids)
    return done[None]


def solution(mesh):
    in_specs = (
        P("queue", None, "mp"),
        P("queue", None, "mp"),
        P("queue", None, "mp"),
        P(None, "mp"),
        P(),
        P("queue"),
        P(),
        P("queue", None),
        P("queue"),
    )
    return jax.shard_map(
        on_device, mesh=mesh, in_specs=in_specs, out_specs=P("queue", None, "mp"), check_vma=False
    )
```
